512 devices in a mesh: depth: 8 (over y), row: 8 (over x, core), col: 8 (over z).
Axes of the slice: x: 4, y: 8, z: 8, core: 2. Of those that a mesh axis runs over, the one named last changes fastest.
Arguments:
- state: float32 [4, 128, 128, 1024], P(None, 'depth', 'row', 'col'), may hold values from 0 to 1
- velocity: float32 [3, 128, 128, 1024], P(None, 'depth', 'row', 'col'), may hold values from -3 to 3
- view_order: int32 [8, 8], P('row', 'col'), may hold values from 0 to 1
- tf_table: int32 [4, 256], replicated, may hold values from 0 to 255
Outputs:
- new_state: float32 [4, 128, 128, 1024], P(None, 'depth', 'row', 'col')
- image: float32 [4, 512, 512], P(None, 'row', 'col')
The draws below stay inside these ranges and needn't reach their ends.
Inputs may be any that keep to these rules, and one draw needn't show every extreme that they name: `view_order`: 0 puts the lowest depth indices in front, 1 the highest. `tf_table`: levels in units of 1/255.
All inputs are finite; a program needn't handle non-finite values.
Results may differ from the reference program's by a relative error of at most 0.0003.
Values sent between devices are 32-bit elements; how exact they have to be, the bound alone decides.
A program may use at most 128 MiB of HBM per device.

```python
import jax
import jax.numpy as jnp
from jax import lax

CR = 16
CC = 128
PIX_R = 64
PIX_C = 64
BINS = 256
ND = 128
NR = 128
NC = 1024
HEIGHT = 512
WIDTH = 512
N_ROW = 8
N_COL = 8


def draw_state(key, part):
    shape = (4, ND, NR, NC)
    first_key = jax.random.fold_in(key, 11)
    second_key = jax.random.fold_in(key, 12)
    chooser = jax.random.uniform(first_key, shape, jnp.float32)
    jitter = jax.random.uniform(second_key, shape, jnp.float32)
    spread = 0.15
    values = jnp.where(chooser >= 0.5, 1.0 - spread * jitter, spread * jitter)
    return jnp.clip(values, 0.0, 1.0).astype(jnp.float32)


def draw_velocity(key, part):
    shape = (3, ND, NR, NC)
    first_key = jax.random.fold_in(key, 21)
    second_key = jax.random.fold_in(key, 22)
    chooser = jax.random.uniform(first_key, shape, jnp.float32)
    magnitude = jax.random.uniform(second_key, shape, jnp.float32, 2.0, 3.0)
    signed = jnp.where(chooser >= 0.5, magnitude, -magnitude)
    return jnp.clip(signed, -3.0, 3.0).astype(jnp.float32)


def with_ends(values, stream_key, smallest, high):
    shape = values.shape
    index_at = [jax.random.randint(jax.random.fold_in(stream_key, axis), (), 0, shape[axis]) for axis in range(len(shape))]
    values = values.at[tuple(index_at)].set(smallest)
    longest = shape.index(max(shape))
    index_at[longest] = (index_at[longest] + 1) % shape[longest]
    return values.at[tuple(index_at)].set(high)


def setup_inputs(seed: int = 0) -> dict:
    key_of = jax.random.split(jax.random.key(seed), 5)
    return {
        "state": draw_state(jax.random.fold_in(key_of[4], 71), 0),
        "velocity": draw_velocity(jax.random.fold_in(key_of[4], 71), 0),
        "view_order": with_ends(jax.random.randint(key_of[2], (N_ROW, N_COL), 0, 2), jax.random.fold_in(key_of[2], 1), 0, 1).astype(jnp.int32),
        "tf_table": with_ends(jax.random.randint(key_of[3], (4, BINS), 0, 256), jax.random.fold_in(key_of[3], 1), 0, 255).astype(jnp.int32),
    }


FIRST_COEF = (0.8, -0.2, 4.0 / 105.0, -1.0 / 280.0)
SECOND_COEF = (1.6, -0.2, 8.0 / 315.0, -1.0 / 560.0)
CENTER_COEF = -205.0 / 72.0
DIFFUSIVITY = (0.05, 0.04, 0.03, 0.08)
TIME_STEP = 0.2
RATE_CONST = 2.0
IGNITION_SLOPE = 8.0
IGNITION_TEMP = 0.5
OXIDIZER_RATIO = 1.5
HEAT_RELEASE = 0.8
SHEAR_CELLS = 2.0
OPACITY_TOTAL = 6.0


def source_terms(centre):
    rate = RATE_CONST * centre[0] * centre[1] * jax.nn.sigmoid(IGNITION_SLOPE * (centre[3] - IGNITION_TEMP))
    return jnp.stack([-rate, -OXIDIZER_RATIO * rate, (1.0 + OXIDIZER_RATIO) * rate, HEAT_RELEASE * rate])


def combine_terms(centre, gradients, laplace, velocity):
    advect = velocity[0][None] * gradients[0] + velocity[1][None] * gradients[1] + velocity[2][None] * gradients[2]
    diffusion = jnp.stack([DIFFUSIVITY[field_index] * laplace[field_index] for field_index in range(4)])
    return diffusion - advect + source_terms(centre)


def tendency(state, velocity):
    laplace = (3.0 * CENTER_COEF) * state
    gradients = []
    for spatial in (1, 2, 3):
        gradient = jnp.zeros_like(state)
        for offset in range(4):
            forward = jnp.roll(state, -(offset + 1), spatial)
            backward = jnp.roll(state, offset + 1, spatial)
            gradient = gradient + FIRST_COEF[offset] * (forward - backward)
            laplace = laplace + SECOND_COEF[offset] * (forward + backward)
        gradients.append(gradient)
    return combine_terms(state, gradients, laplace, velocity)


def row_matrix(slice_total, cell_count, pixels):
    stride = cell_count / pixels
    spread = max(1.0, stride)
    centres = (jnp.arange(pixels, dtype=jnp.float32) + 0.5) * stride - 0.5
    shifts = SHEAR_CELLS * ((jnp.arange(slice_total, dtype=jnp.float32) + 0.5) / slice_total - 0.5)
    places = jnp.clip(centres[None, :] + shifts[:, None], 0.0, cell_count - 1.0)
    cells_at = jnp.arange(cell_count, dtype=jnp.float32)
    return jnp.maximum(0.0, 1.0 - jnp.abs(places[:, :, None] - cells_at[None, None, :]) / spread) / spread


def column_matrix(cell_count, pixels):
    stride = cell_count / pixels
    spread = max(1.0, stride)
    centres = jnp.clip((jnp.arange(pixels, dtype=jnp.float32) + 0.5) * stride - 0.5, 0.0, cell_count - 1.0)
    cells_at = jnp.arange(cell_count, dtype=jnp.float32)
    return jnp.maximum(0.0, 1.0 - jnp.abs(centres[None, :] - cells_at[:, None]) / spread) / spread


def shade_lookup(values, table_values, slice_total):
    levels = table_values.shape[1]
    level = jnp.clip(values, 0.0, 1.0) * (levels - 1.0)
    lower = jnp.clip(jnp.floor(level), 0.0, levels - 2.0)
    fraction = level - lower
    index = lower.astype(jnp.int32)
    below = jnp.take(table_values, index, axis=1)
    above = jnp.take(table_values, index + 1, axis=1)
    raw_colour = (below * (1.0 - fraction)[None, :] + above * fraction[None, :]) * (1.0 / 255.0)
    opacity = (OPACITY_TOTAL / slice_total) * raw_colour[3]
    return jnp.concatenate([opacity[None, :] * raw_colour[:3], opacity[None, :]], 0)


def march_ordered(sampled, table_values, slice_total):
    def advance(running, values):
        accumulated, transmit = running
        colour = shade_lookup(values, table_values, slice_total)
        return (accumulated + transmit[None, :] * colour, transmit * (1.0 - colour[3])), None

    start = (jnp.zeros((4, sampled.shape[1]), jnp.float32), jnp.ones((sampled.shape[1],), jnp.float32))
    finished, unused = lax.scan(advance, start, sampled)
    return finished[0]


def reference(state, velocity, view_order, tf_table):
    first_rate = tendency(state, velocity)
    middle = state + TIME_STEP * first_rate
    second_rate = tendency(middle, velocity)
    new_state = state + (0.5 * TIME_STEP) * (first_rate + second_rate)
    temper = new_state[3].reshape(ND, N_ROW, CR, N_COL, CC)
    row_weights = row_matrix(ND, CR, PIX_R)
    column_weights = column_matrix(CC, PIX_C)
    partial_rows = jnp.einsum("dpr,dirjc->dipjc", row_weights, temper, precision=lax.Precision.HIGHEST)
    sampled = jnp.einsum("dipjc,cq->dipjq", partial_rows, column_weights, precision=lax.Precision.HIGHEST)
    sampled = sampled.reshape(ND, HEIGHT * WIDTH)
    order_map = jnp.broadcast_to(view_order[:, None, :, None], (N_ROW, PIX_R, N_COL, PIX_C)).reshape(HEIGHT * WIDTH)
    ordered = jnp.where(order_map[None, :] == 0, sampled, sampled[::-1])
    table_values = tf_table.astype(jnp.float32)
    image = march_ordered(ordered, table_values, ND)
    return new_state, image.reshape(4, HEIGHT, WIDTH)
```

```python
import functools

import jax
import jax.numpy as jnp
from jax import lax
from jax.experimental import pallas as pl
from jax.experimental.pallas import tpu as pltpu
from jax.sharding import PartitionSpec as P

MESH = pl.DeviceIdType.MESH
FIRST_COEF = (0.8, -0.2, 4.0 / 105.0, -1.0 / 280.0)
SECOND_COEF = (1.6, -0.2, 8.0 / 315.0, -1.0 / 560.0)
CENTER_COEF = -205.0 / 72.0
DIFFUSIVITY = (0.05, 0.04, 0.03, 0.08)
SOURCE = (-1.0, -1.5, 2.5, 0.8)
FIELDS = (3, 0, 1, 2)
ND = 16
NR = 16
LANES = 128
TOP = 8
GROUP = 2
SLICES = 128
PIX = 64


def kernel(sizes, state, velocity, order, table, new_state, image, ext1, ext2, vel, rate, out, pack, got, texture,
           part, mixed, final, in_sem, vel_sem, out_sem, send_sem, recv_sem, part_send, part_recv, fin_send, fin_recv):
    n_depth, n_row, n_col = sizes
    my_depth, my_row, my_col = lax.axis_index("depth"), lax.axis_index("row"), lax.axis_index("col")
    places = {"depth": (my_depth, n_depth), "row": (my_row, n_row), "col": (my_col, n_col)}

    def beside(axis, step):
        at, count = places[axis]
        return {axis: lax.rem(at + step + count, count)}

    barrier = pltpu.get_barrier_semaphore()
    peers = [beside("depth", step) for step in range(1, n_depth)]
    peers += [beside(axis, step) for axis in ("row", "col") for step in (1, -1)]
    for peer in peers:
        pl.semaphore_signal(barrier, inc=1, device_id=peer, device_id_type=MESH)

    def load_field(f):
        return pltpu.make_async_copy(state.at[f], ext1.at[f, 4 : 4 + ND, TOP : TOP + NR, :], in_sem.at[f])

    load_velocity = pltpu.make_async_copy(velocity, vel, vel_sem)
    for f in FIELDS:
        load_field(f).start()
    load_velocity.start()

    lane = lax.broadcasted_iota(jnp.int32, (NR, LANES), 1)
    lane_group = lane // 8

    def remote(stage, f, index, source, target, peer):
        return pltpu.make_async_remote_copy(
            src_ref=source, dst_ref=target, send_sem=send_sem.at[stage, f, index],
            recv_sem=recv_sem.at[stage, f, index], device_id=peer, device_id_type=MESH)

    def face_copies(stage, f):
        if stage == 0:
            source, target, d0, r0 = state, ext1, 0, 0
        else:
            source, target, d0, r0 = ext2, ext2, 4, TOP
        rows, layers = pl.ds(r0, NR), pl.ds(d0, ND)
        return [
            remote(stage, f, 0, source.at[f, pl.ds(d0 + ND - 4, 4), rows, :],
                   target.at[f, 0:4, TOP : TOP + NR, :], beside("depth", 1)),
            remote(stage, f, 1, source.at[f, pl.ds(d0, 4), rows, :],
                   target.at[f, 4 + ND : 8 + ND, TOP : TOP + NR, :], beside("depth", -1)),
            remote(stage, f, 2, source.at[f, layers, pl.ds(r0 + NR - 8, 8), :],
                   target.at[f, 4 : 4 + ND, 0:TOP, :], beside("row", 1)),
            remote(stage, f, 3, source.at[f, layers, pl.ds(r0, 8), :],
                   target.at[f, 4 : 4 + ND, TOP + NR : 2 * TOP + NR, :], beside("row", -1)),
        ]

    def column_copies(stage, f):
        return [
            remote(stage, f, 4, pack.at[stage, f], got.at[stage, 0, f], beside("col", 1)),
            remote(stage, f, 5, pack.at[stage, f], got.at[stage, 1, f], beside("col", -1)),
        ]

    def packed(carry, values, d):
        return jnp.where(lane_group == d, pltpu.roll(values, 4 + 8 * d, 1), carry)

    pl.semaphore_wait(barrier, len(peers))
    for f in FIELDS:
        for copy in face_copies(0, f):
            copy.start()
    for f in FIELDS:
        load_field(f).wait()

        def pack_layer(d, carry):
            return packed(carry, ext1[f, 4 + d, TOP : TOP + NR, :], d)

        pack[0, f] = lax.fori_loop(0, ND, pack_layer, jnp.zeros((NR, LANES), jnp.float32))
        for copy in column_copies(0, f):
            copy.start()

    def rates(ext):
        def one(d, carry):
            where = pl.ds(2 * d, 2)
            body = pl.ds(4 + 2 * d, 2)
            v0, v1, v3 = (ext[f, body, TOP : TOP + NR, :] for f in (0, 1, 3))
            rate[where] = 2.0 * v0 * v1 * jax.nn.sigmoid(8.0 * (v3 - 0.5))
            return carry

        lax.fori_loop(0, ND // 2, one, 0)

    chunk_lane = lax.broadcasted_iota(jnp.int32, (GROUP * NR, LANES), 1)

    def tendency(ext, f, start, border):
        def window(depth_shift, row_shift):
            block = ext[f, pl.ds(start + 4 + depth_shift, GROUP), TOP + row_shift : TOP + NR + row_shift, :]
            return block.reshape(GROUP * NR, LANES)

        centre = window(0, 0)
        edge = jnp.concatenate([pltpu.roll(border, 124 - 8 * (start + i), 1) for i in range(GROUP)], 0)
        laplace = 3.0 * CENTER_COEF * centre
        advect = None
        for spatial in range(3):
            gradient = None
            for offset in range(1, 5):
                if spatial == 0:
                    ahead, behind = window(offset, 0), window(-offset, 0)
                elif spatial == 1:
                    ahead, behind = window(0, offset), window(0, -offset)
                else:
                    ahead = pltpu.roll(jnp.where(chunk_lane < offset, edge, centre), LANES - offset, 1)
                    behind = pltpu.roll(jnp.where(chunk_lane >= LANES - offset, edge, centre), offset, 1)
                term = FIRST_COEF[offset - 1] * (ahead - behind)
                gradient = term if gradient is None else gradient + term
                laplace = laplace + SECOND_COEF[offset - 1] * (ahead + behind)
            flow = vel[spatial, pl.ds(start, GROUP)].reshape(GROUP * NR, LANES)
            advect = flow * gradient if advect is None else advect + flow * gradient
        source = SOURCE[f] * rate[pl.ds(start, GROUP)].reshape(GROUP * NR, LANES)
        return centre, DIFFUSIVITY[f] * laplace - advect + source

    def border_of(stage, f):
        return jnp.where(lane % 8 < 4, got[stage, 0, f], got[stage, 1, f])

    def arrived(stage, f):
        for copy in face_copies(stage, f) + column_copies(stage, f):
            copy.wait_recv()

    rates(ext1)
    load_velocity.wait()
    for f in FIELDS:
        arrived(0, f)
        border = border_of(0, f)

        def first_stage(c, carry):
            start = c * GROUP
            centre, tend = tendency(ext1, f, start, border)
            middle = (centre + 0.2 * tend).reshape(GROUP, NR, LANES)
            ext2[f, pl.ds(start + 4, GROUP), TOP : TOP + NR, :] = middle
            for i in range(GROUP):
                carry = packed(carry, middle[i], start + i)
            return carry

        pack[1, f] = lax.fori_loop(0, ND // GROUP, first_stage, jnp.zeros((NR, LANES), jnp.float32))
        for copy in face_copies(1, f) + column_copies(1, f):
            copy.start()

    rates(ext2)

    def store_field(f):
        return pltpu.make_async_copy(out.at[f], new_state.at[f], out_sem.at[f])

    def second(f):
        arrived(1, f)
        border = border_of(1, f)

        def second_stage(c, carry):
            start = c * GROUP
            centre, tend = tendency(ext2, f, start, border)
            before = ext1[f, pl.ds(start + 4, GROUP), TOP : TOP + NR, :].reshape(GROUP * NR, LANES)
            out[f, pl.ds(start, GROUP)] = (0.5 * (before + centre) + 0.1 * tend).reshape(GROUP, NR, LANES)
            return carry

        lax.fori_loop(0, ND // GROUP, second_stage, 0)
        store_field(f).start()

    second(3)

    from_column = lax.broadcasted_iota(jnp.int32, (LANES, LANES), 0).astype(jnp.float32)
    to_lane = lax.broadcasted_iota(jnp.int32, (LANES, LANES), 1)
    to_column = lax.rem(to_lane, PIX).astype(jnp.float32)
    spot = jnp.clip((to_column + 0.5) * 2.0 - 0.5, 0.0, LANES - 1.0)
    filter_all = jnp.maximum(0.0, 1.0 - jnp.abs(spot - from_column) / 2.0) / 2.0
    for half in range(2):
        part_filter = jnp.where(to_lane // PIX == half, filter_all, 0.0).astype(jnp.bfloat16)
        rest = out[3, half * 8 : half * 8 + 8].reshape(LANES, LANES)
        for piece in range(3):
            coarse = rest.astype(jnp.bfloat16)
            if piece < 2:
                rest = rest - coarse.astype(jnp.float32)
            term = jnp.dot(coarse, part_filter, preferred_element_type=jnp.float32)
            total = term if half == 0 and piece == 0 else total + term
    texture[...] = total

    words = table[0:1, :] + table[1:2, :] * 256 + table[2:3, :] * 65536 + (table[3:4, :] << 24)
    low, high = (jnp.broadcast_to(words[:, i * LANES : (i + 1) * LANES], (8, LANES)) for i in range(2))
    small_lane = lax.broadcasted_iota(jnp.int32, (8, LANES), 1)
    sub = lax.broadcasted_iota(jnp.int32, (8, LANES), 0)
    high_next = pltpu.roll(high, LANES - 1, 1)
    low_next = jnp.where(small_lane == LANES - 1, high_next, pltpu.roll(low, LANES - 1, 1))
    near_half = small_lane < PIX
    lowest_first = jnp.broadcast_to(order[0, 0], (8, LANES)) == 0
    first_half_front = lowest_first == near_half
    far_slice = 8 * (small_lane // PIX)

    def looked_up(sample):
        level = jnp.clip(sample, 0.0, 1.0) * 255.0
        lower = jnp.minimum(jnp.floor(level), 254.0)
        fraction = level - lower
        index = lower.astype(jnp.int32)
        place = index & (LANES - 1)
        upper_half = index >= LANES

        def pick(first, second_table):
            one = jnp.take_along_axis(first, place, axis=1, mode="promise_in_bounds")
            two = jnp.take_along_axis(second_table, place, axis=1, mode="promise_in_bounds")
            return jnp.where(upper_half, two, one)

        below, above = pick(low, high), pick(low_next, high_next)
        channels = []
        for c in range(4):
            b, a = ((lax.shift_right_logical(w, 8 * c) & 255).astype(jnp.float32) for w in (below, above))
            channels.append(b + (a - b) * fraction)
        return channels

    def part_copy(step):
        peer = lax.rem(my_depth + step, n_depth)
        return pltpu.make_async_remote_copy(
            src_ref=part.at[peer], dst_ref=mixed.at[my_depth], send_sem=part_send.at[step],
            recv_sem=part_recv.at[my_depth], device_id={"depth": peer}, device_id_type=MESH)

    def part_arrival(step):
        peer = lax.rem(my_depth + step, n_depth)
        return pltpu.make_async_remote_copy(
            src_ref=part.at[peer], dst_ref=mixed.at[peer], send_sem=part_send.at[step],
            recv_sem=part_recv.at[peer], device_id={"depth": peer}, device_id_type=MESH)

    def final_copy(step):
        peer = lax.rem(my_depth + step, n_depth)
        return pltpu.make_async_remote_copy(
            src_ref=final.at[my_depth], dst_ref=final.at[my_depth], send_sem=fin_send.at[step],
            recv_sem=fin_recv.at[my_depth], device_id={"depth": peer}, device_id_type=MESH)

    def final_arrival(step):
        peer = lax.rem(my_depth + step, n_depth)
        return pltpu.make_async_remote_copy(
            src_ref=final.at[peer], dst_ref=final.at[peer], send_sem=fin_send.at[step],
            recv_sem=fin_recv.at[peer], device_id={"depth": peer}, device_id_type=MESH)

    def rendered(block):
        base = jnp.clip(2 * block - 2 + (2 * my_depth + 5) // 8, 0, NR - 4)
        row = (8 * block + sub).astype(jnp.float32)
        samples = []
        for pair in range(8):
            slice_at = (16 * my_depth + pair + far_slice).astype(jnp.float32)
            spot = jnp.clip((row + 0.5) * 0.25 - 0.5 + 2.0 * ((slice_at + 0.5) / SLICES - 0.5), 0.0, NR - 1.0)
            sample = None
            for i in range(4):
                weight = jnp.maximum(0.0, 1.0 - jnp.abs(spot - (base + i).astype(jnp.float32)))
                term = weight * texture[pl.ds(pair * NR + base + i, 1), :]
                sample = term if sample is None else sample + term
            samples.append(sample)
        clear = jnp.ones((8, LANES), jnp.float32)
        sums = [jnp.zeros((8, LANES), jnp.float32) for _ in range(4)]
        for k in range(8):
            channels = looked_up(jnp.where(lowest_first, samples[k], samples[7 - k]))
            alpha = channels[3] * (6.0 / SLICES / 255.0)
            weight = clear * alpha
            scaled = weight * (1.0 / 255.0)
            for c in range(3):
                sums[c] = sums[c] + scaled * channels[c]
            sums[3] = sums[3] + weight
            clear = clear - weight
        turned = [pltpu.roll(value, PIX, 1) for value in sums]
        front_alpha = jnp.where(first_half_front, sums[3], turned[3])
        pieces = []
        for c in (0, 2):
            near = jnp.where(near_half, sums[c], turned[c + 1])
            far = jnp.where(near_half, turned[c], sums[c + 1])
            front = jnp.where(lowest_first, near, far)
            back = jnp.where(lowest_first, far, near)
            pieces.append(front + (1.0 - front_alpha) * back)
        return pieces

    for step in (4, 3, 5, 2, 6, 1, 7, 0):
        block = lax.rem(my_depth + step, n_depth)
        pieces = rendered(block)
        for i in range(2):
            if step:
                part[block, i] = pieces[i]
            else:
                mixed[my_depth, i] = pieces[i]
        if step:
            part_copy(step).start()

    for f in FIELDS[1:]:
        second(f)

    for step in range(1, n_depth):
        part_arrival(step).wait_recv()
    clear = jnp.ones((8, LANES), jnp.float32)
    sums = [jnp.zeros((8, LANES), jnp.float32) for _ in range(2)]
    for k in range(n_depth):
        pair = [jnp.where(lowest_first, mixed[k, i], mixed[n_depth - 1 - k, i]) for i in range(2)]
        alpha = jnp.where(near_half, pltpu.roll(pair[1], PIX, 1), pair[1])
        sums = [total + clear * value for total, value in zip(sums, pair)]
        clear = clear * (1.0 - alpha)
    for i in range(2):
        final[my_depth, i] = sums[i]
    for step in (4, 3, 5, 2, 6, 1, 7):
        final_copy(step).start()
    for stage in range(2):
        for f in FIELDS:
            for copy in face_copies(stage, f) + column_copies(stage, f):
                copy.wait_send()
    for step in range(1, n_depth):
        part_copy(step).wait_send()
    for f in FIELDS:
        store_field(f).wait()
    for step in range(1, n_depth):
        final_arrival(step).wait_recv()
    for block in range(n_depth):
        for i in range(2):
            value = final[block, i]
            image[2 * i, 8 * block : 8 * block + 8, :] = value[:, :PIX]
            image[2 * i + 1, 8 * block : 8 * block + 8, :] = value[:, PIX:]
    for step in range(1, n_depth):
        final_copy(step).wait_send()


def solution(mesh):
    sizes = tuple(mesh.shape[axis] for axis in ("depth", "row", "col"))
    f32 = jnp.float32
    any_space = pl.BlockSpec(memory_space=pl.ANY)
    vmem = pl.BlockSpec(memory_space=pltpu.VMEM)
    smem = pl.BlockSpec(memory_space=pltpu.SMEM)
    extended = (4, ND + 8, NR + 16, LANES)

    def local(state, velocity, view_order, tf_table):
        return tuple(pl.pallas_call(
            functools.partial(kernel, sizes),
            out_shape=(
                jax.ShapeDtypeStruct((4, ND, NR, LANES), f32),
                jax.ShapeDtypeStruct((4, PIX, PIX), f32),
            ),
            in_specs=[any_space, any_space, smem, vmem],
            out_specs=(any_space, vmem),
            scratch_shapes=[
                pltpu.VMEM(extended, f32),
                pltpu.VMEM(extended, f32),
                pltpu.VMEM((3, ND, NR, LANES), f32),
                pltpu.VMEM((ND, NR, LANES), f32),
                pltpu.VMEM((4, ND, NR, LANES), f32),
                pltpu.VMEM((2, 4, NR, LANES), f32),
                pltpu.VMEM((2, 2, 4, NR, LANES), f32),
                pltpu.VMEM((LANES, LANES), f32),
                pltpu.VMEM((8, 2, 8, LANES), f32),
                pltpu.VMEM((8, 2, 8, LANES), f32),
                pltpu.VMEM((8, 2, 8, LANES), f32),
                pltpu.SemaphoreType.DMA((4,)),
                pltpu.SemaphoreType.DMA,
                pltpu.SemaphoreType.DMA((4,)),
                pltpu.SemaphoreType.DMA((2, 4, 6)),
                pltpu.SemaphoreType.DMA((2, 4, 6)),
                pltpu.SemaphoreType.DMA((8,)),
                pltpu.SemaphoreType.DMA((8,)),
                pltpu.SemaphoreType.DMA((8,)),
                pltpu.SemaphoreType.DMA((8,)),
            ],
            compiler_params=pltpu.CompilerParams(collective_id=0, has_side_effects=True),
        )(state, velocity, view_order, tf_table))

    return jax.shard_map(
        local,
        mesh=mesh,
        in_specs=(P(None, "depth", "row", "col"), P(None, "depth", "row", "col"), P("row", "col"), P()),
        out_specs=(P(None, "depth", "row", "col"), P(None, "row", "col")),
        check_vma=False,
    )
```

```python
import functools

import jax
import jax.numpy as jnp
from jax import lax
from jax.experimental import pallas as pl
from jax.experimental.pallas import tpu as pltpu
from jax.sharding import PartitionSpec as P

MESH = pl.DeviceIdType.MESH
FIRST_COEF = (0.8, -0.2, 4.0 / 105.0, -1.0 / 280.0)
SECOND_COEF = (1.6, -0.2, 8.0 / 315.0, -1.0 / 560.0)
CENTER_COEF = -205.0 / 72.0
DIFFUSIVITY = (0.05, 0.04, 0.03, 0.08)
SOURCE = (-1.0, -1.5, 2.5, 0.8)
FIELDS = (3, 0, 1, 2)
ND = 16
NR = 16
LANES = 128
TOP = 8
CHUNK = 4
ROWS = CHUNK * NR
SLICES = 128
PIX = 64


def kernel(sizes, state, velocity, order_in, table_in, new_state, image, ext1, ext2, vel, rate, partial, out, pack, got,
           flow_pack, weights, filters, words, order, table, texture, part, mixed, final, in_sem, vel_sem, small_sem, out_sem,
           send_sem, recv_sem, part_send, part_recv, fin_send, fin_recv, token):
    n_depth, n_row, n_col = sizes
    my_depth, my_row, my_col = lax.axis_index("depth"), lax.axis_index("row"), lax.axis_index("col")
    places = {"depth": (my_depth, n_depth), "row": (my_row, n_row), "col": (my_col, n_col)}

    def beside(axis, step):
        at, count = places[axis]
        return {axis: lax.rem(at + step + count, count)}

    barrier = pltpu.get_barrier_semaphore()
    neighbours = [beside(axis, step) for axis in ("depth", "row", "col") for step in (1, -1)]
    for peer in neighbours:
        pl.semaphore_signal(barrier, inc=1, device_id=peer, device_id_type=MESH)

    def load_field(f):
        return pltpu.make_async_copy(state.at[f], ext1.at[f, 4 : 4 + ND, TOP : TOP + NR, :], in_sem.at[f])

    load_velocity = pltpu.make_async_copy(velocity, vel, vel_sem)
    load_order = pltpu.make_async_copy(order_in, order, small_sem.at[0])
    load_table = pltpu.make_async_copy(table_in, table, small_sem.at[1])
    for f in FIELDS:
        load_field(f).start()
    load_velocity.start()
    load_order.start()
    load_table.start()

    lane = lax.broadcasted_iota(jnp.int32, (NR, LANES), 1)
    chunk_lane = lax.broadcasted_iota(jnp.int32, (ROWS, LANES), 1)
    chunk_edge = (chunk_lane < 4) | (chunk_lane >= LANES - 4)
    small_lane = lax.broadcasted_iota(jnp.int32, (8, LANES), 1)
    sub = lax.broadcasted_iota(jnp.int32, (8, LANES), 0)
    near_half = small_lane < PIX
    in_group = lane & 7
    low_side = in_group < 4

    def row_base(block):
        return jnp.clip(2 * block - 2 + (2 * my_depth + 5) // 8, 0, NR - 4)

    far_slice = 8 * (small_lane // PIX)
    for block in range(8):
        base = row_base(block)
        row = (8 * block + sub).astype(jnp.float32)
        slice_at = (16 * my_depth + far_slice).astype(jnp.float32)
        first_spot = (row + 0.5) * 0.25 - 0.5 + 2.0 * ((slice_at + 0.5) / SLICES - 0.5)
        for pair in range(8):
            spot = jnp.clip(first_spot + pair * (2.0 / SLICES), 0.0, NR - 1.0) - base.astype(jnp.float32)
            for i in range(4):
                weights[block, pair, i] = jnp.maximum(0.0, 1.0 - jnp.abs(spot - float(i)))
    from_column = lax.broadcasted_iota(jnp.int32, (LANES, LANES), 0).astype(jnp.float32)
    to_lane = lax.broadcasted_iota(jnp.int32, (LANES, LANES), 1)
    to_column = (to_lane & (PIX - 1)).astype(jnp.float32)
    spot = jnp.clip((to_column + 0.5) * 2.0 - 0.5, 0.0, LANES - 1.0)
    filter_all = jnp.maximum(0.0, 1.0 - jnp.abs(spot - from_column) / 2.0) / 2.0
    for half in range(2):
        filters[half] = jnp.where(to_lane // PIX == half, filter_all, 0.0).astype(jnp.bfloat16)

    def remote(stage, f, index, source, target, peer):
        return pltpu.make_async_remote_copy(
            src_ref=source, dst_ref=target, send_sem=send_sem.at[stage, f, index],
            recv_sem=recv_sem.at[stage, f, index], device_id=peer, device_id_type=MESH)

    def face_copies(stage, f):
        if stage == 0:
            source, target, d0, r0 = state, ext1, 0, 0
        else:
            source, target, d0, r0 = ext2, ext2, 4, TOP
        rows, layers = pl.ds(r0, NR), pl.ds(d0, ND)
        return [
            remote(stage, f, 0, source.at[f, pl.ds(d0 + ND - 4, 4), rows, :],
                   target.at[f, 0:4, TOP : TOP + NR, :], beside("depth", 1)),
            remote(stage, f, 1, source.at[f, pl.ds(d0, 4), rows, :],
                   target.at[f, 4 + ND : 8 + ND, TOP : TOP + NR, :], beside("depth", -1)),
            remote(stage, f, 2, source.at[f, layers, pl.ds(r0 + NR - 8, 8), :],
                   target.at[f, 4 : 4 + ND, 0:TOP, :], beside("row", 1)),
            remote(stage, f, 3, source.at[f, layers, pl.ds(r0, 8), :],
                   target.at[f, 4 : 4 + ND, TOP + NR : 2 * TOP + NR, :], beside("row", -1)),
        ]

    def column_copies(stage, f):
        return [
            remote(stage, f, 4, pack.at[stage, f], got.at[stage, 0, f], beside("col", 1)),
            remote(stage, f, 5, pack.at[stage, f], got.at[stage, 1, f], beside("col", -1)),
        ]

    lane_group = lane // 8

    def packed(layers):
        gathered = None
        for d, values in enumerate(layers):
            turned = pltpu.roll(values, (4 + 8 * d) % LANES, 1)
            gathered = turned if d == 0 else jnp.where(lane_group == d, turned, gathered)
        return gathered

    def body(ext, f, d):
        return ext[f, 4 + d, TOP : TOP + NR, :]

    pl.semaphore_wait(barrier, len(neighbours))
    for f in FIELDS:
        for copy in face_copies(0, f):
            copy.start()
    for f in FIELDS:
        load_field(f).wait()
        pack[0, f] = packed([body(ext1, f, d) for d in range(ND)])
        for copy in column_copies(0, f):
            copy.start()

    def rates(ext):
        for d in range(0, ND, CHUNK):
            v0, v1, v3 = (ext[f, 4 + d : 4 + d + CHUNK, TOP : TOP + NR, :] for f in (0, 1, 3))
            rate[d : d + CHUNK] = 2.0 * v0 * v1 * jax.nn.sigmoid(8.0 * (v3 - 0.5))

    def flow(spatial, d):
        return vel[spatial, d : d + CHUNK].reshape(ROWS, LANES)

    def columns_part(ext, f):
        for d in range(0, ND, CHUNK):
            centre = ext[f, 4 + d : 4 + d + CHUNK, TOP : TOP + NR, :].reshape(ROWS, LANES)
            total = (3.0 * CENTER_COEF * DIFFUSIVITY[f]) * centre
            gradient = None
            for offset in range(1, 5):
                ahead, behind = pltpu.roll(centre, LANES - offset, 1), pltpu.roll(centre, offset, 1)
                term = FIRST_COEF[offset - 1] * (ahead - behind)
                gradient = term if gradient is None else gradient + term
                total = total + (SECOND_COEF[offset - 1] * DIFFUSIVITY[f]) * (ahead + behind)
            partial[f, d : d + CHUNK] = (total - flow(2, d) * gradient).reshape(CHUNK, NR, LANES)

    def edge_terms(stage, f):
        change = jnp.where(low_side, got[stage, 0, f], got[stage, 1, f]) - pack[stage, f]
        second = first = None
        for offset in range(1, 5):
            ahead, behind = pltpu.roll(change, LANES - offset, 1), pltpu.roll(change, offset, 1)
            reach = (low_side & (in_group + offset >= 4)) | ((in_group >= 4) & (in_group - offset <= 3))
            moved = jnp.where(reach, jnp.where(low_side, ahead, behind), 0.0)
            one, two = FIRST_COEF[offset - 1] * moved, (SECOND_COEF[offset - 1] * DIFFUSIVITY[f]) * moved
            first = one if first is None else first + one
            second = two if second is None else second + two
        first = jnp.where(low_side, first, -first)
        return second - flow_pack[...] * first

    def tendency(ext, f, edges, d):
        def window(depth_shift, row_shift):
            d0, r0 = d + 4 + depth_shift, TOP + row_shift
            return ext[f, d0 : d0 + CHUNK, r0 : r0 + NR, :].reshape(ROWS, LANES)

        total = partial[f, d : d + CHUNK].reshape(ROWS, LANES)
        total = total + SOURCE[f] * rate[d : d + CHUNK].reshape(ROWS, LANES)
        along_depth = along_rows = None
        for offset in range(1, 5):
            up, down = window(offset, 0), window(-offset, 0)
            ahead, behind = window(0, offset), window(0, -offset)
            total = total + (SECOND_COEF[offset - 1] * DIFFUSIVITY[f]) * ((up + down) + (ahead + behind))
            one, two = FIRST_COEF[offset - 1] * (up - down), FIRST_COEF[offset - 1] * (ahead - behind)
            along_depth = one if along_depth is None else along_depth + one
            along_rows = two if along_rows is None else along_rows + two
        total = total - (flow(0, d) * along_depth + flow(1, d) * along_rows)
        edge = jnp.concatenate([pltpu.roll(edges, (124 - 8 * (d + i)) % LANES, 1) for i in range(CHUNK)], 0)
        return window(0, 0), total + jnp.where(chunk_edge, edge, 0.0)

    def arrived(stage, f):
        for copy in face_copies(stage, f) + column_copies(stage, f):
            copy.wait_recv()

    load_velocity.wait()
    flow_pack[...] = packed([vel[2, d] for d in range(ND)])
    columns_part(ext1, 3)
    rates(ext1)
    for f in FIELDS[1:]:
        columns_part(ext1, f)

    def first_stage(f):
        arrived(0, f)
        edges = edge_terms(0, f)
        for d in range(0, ND, CHUNK):
            centre, tend = tendency(ext1, f, edges, d)
            ext2[f, 4 + d : 4 + d + CHUNK, TOP : TOP + NR, :] = (centre + 0.2 * tend).reshape(CHUNK, NR, LANES)
        for copy in face_copies(1, f):
            copy.start()
        pack[1, f] = packed([body(ext2, f, d) for d in range(ND)])
        for copy in column_copies(1, f):
            copy.start()

    for f in FIELDS:
        first_stage(f)
    columns_part(ext2, 3)
    rates(ext2)

    load_order.wait()
    load_table.wait()
    word = table[0:1, :] + table[1:2, :] * 256 + table[2:3, :] * 65536 + (table[3:4, :] << 24)
    low, high = (jnp.broadcast_to(word[:, i * LANES : (i + 1) * LANES], (8, LANES)) for i in range(2))
    high_next = pltpu.roll(high, LANES - 1, 1)
    words[0] = low
    words[1] = high
    words[2] = jnp.where(small_lane == LANES - 1, high_next, pltpu.roll(low, LANES - 1, 1))
    words[3] = high_next
    lowest_first = jnp.broadcast_to(order[...], (8, LANES)) == 0
    first_half_front = lowest_first == near_half

    def store_field(f):
        return pltpu.make_async_copy(out.at[f], new_state.at[f], out_sem.at[f])

    def second_stage(f):
        edges = edge_terms(1, f)
        for d in range(0, ND, CHUNK):
            centre, tend = tendency(ext2, f, edges, d)
            before = ext1[f, 4 + d : 4 + d + CHUNK, TOP : TOP + NR, :].reshape(ROWS, LANES)
            out[f, d : d + CHUNK] = (0.5 * (before + centre) + 0.1 * tend).reshape(CHUNK, NR, LANES)
        store_field(f).start()

    arrived(1, 3)
    for side, peer in enumerate((beside("depth", 1), beside("depth", -1))):
        pl.semaphore_signal(token.at[side], inc=1, device_id=peer, device_id_type=MESH)
    second_stage(3)

    total = None
    for half in range(2):
        rest = out[3, half * 8 : half * 8 + 8].reshape(LANES, LANES)
        for piece in range(3):
            coarse = rest.astype(jnp.bfloat16)
            if piece < 2:
                rest = rest - coarse.astype(jnp.float32)
            term = jnp.dot(coarse, filters[half], preferred_element_type=jnp.float32)
            total = term if total is None else total + term
    texture[...] = total * 255.0

    def looked_up(sample):
        level = jnp.clip(sample, 0.0, 255.0)
        index = jnp.minimum(level.astype(jnp.int32), 254)
        fraction = level - index.astype(jnp.float32)
        place = index & (LANES - 1)
        upper_half = index >= LANES

        def pick(first):
            one = jnp.take_along_axis(words[first], place, axis=1, mode="promise_in_bounds")
            two = jnp.take_along_axis(words[first + 1], place, axis=1, mode="promise_in_bounds")
            return jnp.where(upper_half, two, one)

        def channels(value):
            spread = [value & 255, lax.shift_right_logical(value, 8) & 255, lax.shift_right_logical(value, 16) & 255,
                      lax.shift_right_logical(value, 24)]
            return [channel.astype(jnp.float32) for channel in spread]

        return channels(pick(0)), channels(pick(2)), fraction

    def peer_at(step):
        return lax.rem(my_depth + step, n_depth)

    def part_copy(step):
        peer = peer_at(step)
        return pltpu.make_async_remote_copy(
            src_ref=part.at[peer], dst_ref=mixed.at[my_depth], send_sem=part_send.at[step],
            recv_sem=part_recv.at[my_depth], device_id={"depth": peer}, device_id_type=MESH)

    def part_arrival(step):
        peer = peer_at(step)
        return pltpu.make_async_remote_copy(
            src_ref=part.at[peer], dst_ref=mixed.at[peer], send_sem=part_send.at[step],
            recv_sem=part_recv.at[peer], device_id={"depth": peer}, device_id_type=MESH)

    def final_copy(step):
        peer = peer_at(step)
        return pltpu.make_async_remote_copy(
            src_ref=final.at[my_depth], dst_ref=final.at[my_depth], send_sem=fin_send.at[step],
            recv_sem=fin_recv.at[my_depth], device_id={"depth": peer}, device_id_type=MESH)

    def final_arrival(step):
        peer = peer_at(step)
        return pltpu.make_async_remote_copy(
            src_ref=final.at[peer], dst_ref=final.at[peer], send_sem=fin_send.at[step],
            recv_sem=fin_recv.at[peer], device_id={"depth": peer}, device_id_type=MESH)

    def rendered(block):
        base = row_base(block)
        samples = []
        for pair in range(8):
            sample = None
            for i in range(4):
                term = weights[block, pair, i] * texture[pl.ds(pair * NR + base + i, 1), :]
                sample = term if sample is None else sample + term
            samples.append(sample)
        clear = jnp.ones((8, LANES), jnp.float32)
        sums = [jnp.zeros((8, LANES), jnp.float32) for _ in range(3)]
        for k in range(8):
            below, above, fraction = looked_up(jnp.where(lowest_first, samples[k], samples[7 - k]))
            alpha = (below[3] + (above[3] - below[3]) * fraction) * (6.0 / SLICES / 255.0)
            weight = clear * alpha
            share = weight * fraction
            keep = weight - share
            for c in range(3):
                sums[c] = sums[c] + (keep * below[c] + share * above[c])
            clear = clear - weight
        sums = [value * (1.0 / 255.0) for value in sums] + [1.0 - clear]
        turned = [pltpu.roll(value, PIX, 1) for value in sums]
        front_alpha = jnp.where(first_half_front, sums[3], turned[3])
        pieces = []
        for c in (0, 2):
            near = jnp.where(near_half, sums[c], turned[c + 1])
            far = jnp.where(near_half, turned[c], sums[c + 1])
            front = jnp.where(lowest_first, near, far)
            back = jnp.where(lowest_first, far, near)
            pieces.append(front + (1.0 - front_alpha) * back)
        return pieces

    for step in (4, 3, 5, 2, 6, 1, 7, 0):
        block = peer_at(step)
        pieces = rendered(block)
        for i in range(2):
            if step:
                part[block, i] = pieces[i]
            else:
                mixed[my_depth, i] = pieces[i]
        if step == 4:
            for side in range(2):
                pl.semaphore_wait(token.at[side], 1)
        if step:
            part_copy(step).start()

    for f in FIELDS[1:]:
        columns_part(ext2, f)
        arrived(1, f)
        second_stage(f)

    for step in range(1, n_depth):
        part_arrival(step).wait_recv()
    clear = jnp.ones((8, LANES), jnp.float32)
    sums = [jnp.zeros((8, LANES), jnp.float32) for _ in range(2)]
    for k in range(n_depth):
        pair = [jnp.where(lowest_first, mixed[k, i], mixed[n_depth - 1 - k, i]) for i in range(2)]
        alpha = jnp.where(near_half, pltpu.roll(pair[1], PIX, 1), pair[1])
        sums = [total + clear * value for total, value in zip(sums, pair)]
        clear = clear * (1.0 - alpha)
    for i in range(2):
        final[my_depth, i] = sums[i]
    for step in (4, 3, 5, 2, 6, 1, 7):
        final_copy(step).start()
    for stage in range(2):
        for f in FIELDS:
            for copy in face_copies(stage, f) + column_copies(stage, f):
                copy.wait_send()
    for step in range(1, n_depth):
        part_copy(step).wait_send()
    for f in FIELDS:
        store_field(f).wait()
    for step in range(1, n_depth):
        final_arrival(step).wait_recv()
    for block in range(n_depth):
        for i in range(2):
            value = final[block, i]
            image[2 * i, 8 * block : 8 * block + 8, :] = value[:, :PIX]
            image[2 * i + 1, 8 * block : 8 * block + 8, :] = value[:, PIX:]
    for step in range(1, n_depth):
        final_copy(step).wait_send()


def solution(mesh):
    sizes = tuple(mesh.shape[axis] for axis in ("depth", "row", "col"))
    f32 = jnp.float32
    any_space = pl.BlockSpec(memory_space=pl.ANY)
    vmem = pl.BlockSpec(memory_space=pltpu.VMEM)
    extended = (4, ND + 8, NR + 16, LANES)

    def local(state, velocity, view_order, tf_table):
        return tuple(pl.pallas_call(
            functools.partial(kernel, sizes),
            out_shape=(
                jax.ShapeDtypeStruct((4, ND, NR, LANES), f32),
                jax.ShapeDtypeStruct((4, PIX, PIX), f32),
            ),
            in_specs=[any_space] * 4,
            out_specs=(any_space, vmem),
            scratch_shapes=[
                pltpu.VMEM(extended, f32),
                pltpu.VMEM(extended, f32),
                pltpu.VMEM((3, ND, NR, LANES), f32),
                pltpu.VMEM((ND, NR, LANES), f32),
                pltpu.VMEM((4, ND, NR, LANES), f32),
                pltpu.VMEM((4, ND, NR, LANES), f32),
                pltpu.VMEM((2, 4, NR, LANES), f32),
                pltpu.VMEM((2, 2, 4, NR, LANES), f32),
                pltpu.VMEM((NR, LANES), f32),
                pltpu.VMEM((8, 8, 4, 8, LANES), f32),
                pltpu.VMEM((2, LANES, LANES), jnp.bfloat16),
                pltpu.VMEM((4, 8, LANES), jnp.int32),
                pltpu.VMEM((1, 1), jnp.int32),
                pltpu.VMEM((4, 2 * LANES), jnp.int32),
                pltpu.VMEM((LANES, LANES), f32),
                pltpu.VMEM((8, 2, 8, LANES), f32),
                pltpu.VMEM((8, 2, 8, LANES), f32),
                pltpu.VMEM((8, 2, 8, LANES), f32),
                pltpu.SemaphoreType.DMA((4,)),
                pltpu.SemaphoreType.DMA,
                pltpu.SemaphoreType.DMA((2,)),
                pltpu.SemaphoreType.DMA((4,)),
                pltpu.SemaphoreType.DMA((2, 4, 6)),
                pltpu.SemaphoreType.DMA((2, 4, 6)),
                pltpu.SemaphoreType.DMA((8,)),
                pltpu.SemaphoreType.DMA((8,)),
                pltpu.SemaphoreType.DMA((8,)),
                pltpu.SemaphoreType.DMA((8,)),
                pltpu.SemaphoreType.REGULAR((2,)),
            ],
            compiler_params=pltpu.CompilerParams(collective_id=0, has_side_effects=True),
        )(state, velocity, view_order, tf_table))

    return jax.shard_map(
        local,
        mesh=mesh,
        in_specs=(P(None, "depth", "row", "col"), P(None, "depth", "row", "col"), P("row", "col"), P()),
        out_specs=(P(None, "depth", "row", "col"), P(None, "row", "col")),
        check_vma=False,
    )
```

```python
import functools

import jax
import jax.numpy as jnp
from jax import lax
from jax.experimental import pallas as pl
from jax.experimental.pallas import tpu as pltpu
from jax.sharding import PartitionSpec as P

MESH = pl.DeviceIdType.MESH
FIRST_COEF = (0.8, -0.2, 4.0 / 105.0, -1.0 / 280.0)
SECOND_COEF = (1.6, -0.2, 8.0 / 315.0, -1.0 / 560.0)
CENTER_COEF = -205.0 / 72.0
DIFFUSIVITY = (0.05, 0.04, 0.03, 0.08)
SOURCE = (-1.0, -1.5, 2.5, 0.8)
FIELDS = (3, 0, 1, 2)
ND = 16
NR = 16
LANES = 128
TOP = 8
CHUNK = 4
ROWS = CHUNK * NR
SLICES = 128
PIX = 64


def kernel(sizes, state, velocity, order_in, table_in, out, final, ext1, ext2, vel, rate, partial, pack, got,
           flow_pack, weights, filters, words, order, table, texture, part, mixed, in_sem, vel_sem, small_sem,
           send_sem, recv_sem, part_send, part_recv, fin_send, fin_recv, token):
    n_depth, n_row, n_col = sizes
    my_depth, my_row, my_col = lax.axis_index("depth"), lax.axis_index("row"), lax.axis_index("col")
    places = {"depth": (my_depth, n_depth), "row": (my_row, n_row), "col": (my_col, n_col)}

    def beside(axis, step):
        at, count = places[axis]
        return {axis: lax.rem(at + step + count, count)}

    barrier = pltpu.get_barrier_semaphore()
    neighbours = [beside(axis, step) for axis in ("depth", "row", "col") for step in (1, -1)]
    for peer in neighbours:
        pl.semaphore_signal(barrier, inc=1, device_id=peer, device_id_type=MESH)

    def load_field(f):
        return pltpu.make_async_copy(state.at[f], ext1.at[f, 4 : 4 + ND, TOP : TOP + NR, :], in_sem.at[f])

    load_velocity = pltpu.make_async_copy(velocity, vel, vel_sem)
    load_order = pltpu.make_async_copy(order_in, order, small_sem.at[0])
    load_table = pltpu.make_async_copy(table_in, table, small_sem.at[1])
    for f in FIELDS:
        load_field(f).start()
    load_velocity.start()
    load_order.start()
    load_table.start()

    lane = lax.broadcasted_iota(jnp.int32, (NR, LANES), 1)
    chunk_lane = lax.broadcasted_iota(jnp.int32, (ROWS, LANES), 1)
    chunk_edge = (chunk_lane < 4) | (chunk_lane >= LANES - 4)
    small_lane = lax.broadcasted_iota(jnp.int32, (8, LANES), 1)
    sub = lax.broadcasted_iota(jnp.int32, (8, LANES), 0)
    near_half = small_lane < PIX
    in_group = lane & 7
    low_side = in_group < 4

    def row_base(block):
        return jnp.clip(2 * block - 2 + (2 * my_depth + 5) // 8, 0, NR - 4)

    def remote(stage, f, index, source, target, peer):
        return pltpu.make_async_remote_copy(
            src_ref=source, dst_ref=target, send_sem=send_sem.at[stage, f, index],
            recv_sem=recv_sem.at[stage, f, index], device_id=peer, device_id_type=MESH)

    def face_copies(stage, f):
        if stage == 0:
            source, target, d0, r0 = state, ext1, 0, 0
        else:
            source, target, d0, r0 = ext2, ext2, 4, TOP
        rows, layers = pl.ds(r0, NR), pl.ds(d0, ND)
        return [
            remote(stage, f, 0, source.at[f, pl.ds(d0 + ND - 4, 4), rows, :],
                   target.at[f, 0:4, TOP : TOP + NR, :], beside("depth", 1)),
            remote(stage, f, 1, source.at[f, pl.ds(d0, 4), rows, :],
                   target.at[f, 4 + ND : 8 + ND, TOP : TOP + NR, :], beside("depth", -1)),
            remote(stage, f, 2, source.at[f, layers, pl.ds(r0 + NR - 4, 4), :],
                   target.at[f, 4 : 4 + ND, TOP - 4 : TOP, :], beside("row", 1)),
            remote(stage, f, 3, source.at[f, layers, pl.ds(r0, 4), :],
                   target.at[f, 4 : 4 + ND, TOP + NR : TOP + NR + 4, :], beside("row", -1)),
        ]

    def column_copies(stage, f):
        return [
            remote(stage, f, 4, pack.at[stage, f], got.at[stage, 0, f], beside("col", 1)),
            remote(stage, f, 5, pack.at[stage, f], got.at[stage, 1, f], beside("col", -1)),
        ]

    lane_group = lane // 8

    def packed(layers):
        gathered = None
        for d, values in enumerate(layers):
            turned = pltpu.roll(values, (4 + 8 * d) % LANES, 1)
            gathered = turned if d == 0 else jnp.where(lane_group == d, turned, gathered)
        return gathered

    def body(ext, f, d):
        return ext[f, 4 + d, TOP : TOP + NR, :]

    pl.semaphore_wait(barrier, len(neighbours))
    def rates(ext, stage):
        for d in range(0, ND, CHUNK):
            v0, v1, v3 = (ext[f, 4 + d : 4 + d + CHUNK, TOP : TOP + NR, :] for f in (0, 1, 3))
            rate[stage, d : d + CHUNK] = 2.0 * v0 * v1 * jax.nn.sigmoid(8.0 * (v3 - 0.5))

    def flow(spatial, d):
        return vel[spatial, d : d + CHUNK].reshape(ROWS, LANES)

    def columns_part(ext, f):
        for d in range(0, ND, CHUNK):
            centre = ext[f, 4 + d : 4 + d + CHUNK, TOP : TOP + NR, :].reshape(ROWS, LANES)
            total = (3.0 * CENTER_COEF * DIFFUSIVITY[f]) * centre
            gradient = None
            for offset in range(1, 5):
                ahead, behind = pltpu.roll(centre, LANES - offset, 1), pltpu.roll(centre, offset, 1)
                term = FIRST_COEF[offset - 1] * (ahead - behind)
                gradient = term if gradient is None else gradient + term
                total = total + (SECOND_COEF[offset - 1] * DIFFUSIVITY[f]) * (ahead + behind)
            partial[f, d : d + CHUNK] = (total - flow(2, d) * gradient).reshape(CHUNK, NR, LANES)

    def edge_terms(stage, f):
        change = jnp.where(low_side, got[stage, 0, f], got[stage, 1, f]) - pack[stage, f]
        second = first = None
        for offset in range(1, 5):
            ahead, behind = pltpu.roll(change, LANES - offset, 1), pltpu.roll(change, offset, 1)
            reach = (low_side & (in_group + offset >= 4)) | ((in_group >= 4) & (in_group - offset <= 3))
            moved = jnp.where(reach, jnp.where(low_side, ahead, behind), 0.0)
            one, two = FIRST_COEF[offset - 1] * moved, (SECOND_COEF[offset - 1] * DIFFUSIVITY[f]) * moved
            first = one if first is None else first + one
            second = two if second is None else second + two
        first = jnp.where(low_side, first, -first)
        return second - flow_pack[...] * first

    def tendency(stage, f, edges, d):
        ext = (ext1, ext2)[stage]

        def window(depth_shift, row_shift):
            d0, r0 = d + 4 + depth_shift, TOP + row_shift
            return ext[f, d0 : d0 + CHUNK, r0 : r0 + NR, :].reshape(ROWS, LANES)

        total = partial[f, d : d + CHUNK].reshape(ROWS, LANES)
        total = total + SOURCE[f] * rate[stage, d : d + CHUNK].reshape(ROWS, LANES)
        along_depth = along_rows = None
        for offset in range(1, 5):
            up, down = window(offset, 0), window(-offset, 0)
            ahead, behind = window(0, offset), window(0, -offset)
            total = total + (SECOND_COEF[offset - 1] * DIFFUSIVITY[f]) * ((up + down) + (ahead + behind))
            one, two = FIRST_COEF[offset - 1] * (up - down), FIRST_COEF[offset - 1] * (ahead - behind)
            along_depth = one if along_depth is None else along_depth + one
            along_rows = two if along_rows is None else along_rows + two
        total = total - (flow(0, d) * along_depth + flow(1, d) * along_rows)
        edge = jnp.concatenate([pltpu.roll(edges, (124 - 8 * (d + i)) % LANES, 1) for i in range(CHUNK)], 0)
        return window(0, 0), total + jnp.where(chunk_edge, edge, 0.0)

    def arrived(stage, f, indices):
        copies = face_copies(stage, f) + column_copies(stage, f)
        for index in indices:
            copies[index].wait_recv()

    def prepare():
        far_slice = 8 * (small_lane // PIX)
        for block in range(8):
            base = row_base(block)
            row = (8 * block + sub).astype(jnp.float32)
            slice_at = (16 * my_depth + far_slice).astype(jnp.float32)
            first_spot = (row + 0.5) * 0.25 - 0.5 + 2.0 * ((slice_at + 0.5) / SLICES - 0.5)
            for pair in range(8):
                spot = jnp.clip(first_spot + pair * (2.0 / SLICES), 0.0, NR - 1.0) - base.astype(jnp.float32)
                for i in range(4):
                    weights[block, pair, i] = jnp.maximum(0.0, 1.0 - jnp.abs(spot - float(i)))
        from_column = lax.broadcasted_iota(jnp.int32, (LANES, LANES), 0).astype(jnp.float32)
        to_lane = lax.broadcasted_iota(jnp.int32, (LANES, LANES), 1)
        to_column = (to_lane & (PIX - 1)).astype(jnp.float32)
        spot = jnp.clip((to_column + 0.5) * 2.0 - 0.5, 0.0, LANES - 1.0)
        filter_all = jnp.maximum(0.0, 1.0 - jnp.abs(spot - from_column) / 2.0) / 2.0
        for half in range(2):
            filters[half] = jnp.where(to_lane // PIX == half, filter_all, 0.0).astype(jnp.bfloat16)

    def send_first(f):
        for copy in face_copies(0, f):
            copy.start()
        load_field(f).wait()
        pack[0, f] = packed([body(ext1, f, d) for d in range(ND)])
        for copy in column_copies(0, f):
            copy.start()

    send_first(3)
    load_velocity.wait()
    flow_pack[...] = packed([vel[2, d] for d in range(ND)])
    columns_part(ext1, 3)
    send_first(0)
    columns_part(ext1, 0)
    send_first(1)
    rates(ext1, 0)
    columns_part(ext1, 1)
    prepare()

    def first_stage(f):
        arrived(0, f, (2, 3, 4, 5))
        edges = edge_terms(0, f)

        def layers(d):
            centre, tend = tendency(0, f, edges, d)
            ext2[f, 4 + d : 4 + d + CHUNK, TOP : TOP + NR, :] = (centre + 0.2 * tend).reshape(CHUNK, NR, LANES)

        copies = face_copies(1, f)
        for d in range(CHUNK, ND - CHUNK, CHUNK):
            layers(d)
        arrived(0, f, (0, 1))
        layers(0)
        copies[1].start()
        layers(ND - CHUNK)
        for index in (0, 2, 3):
            copies[index].start()
        pack[1, f] = packed([body(ext2, f, d) for d in range(ND)])
        for copy in column_copies(1, f):
            copy.start()

    first_stage(3)
    send_first(2)
    first_stage(0)
    first_stage(1)
    columns_part(ext2, 3)
    rates(ext2, 1)

    load_order.wait()
    load_table.wait()
    word = table[0:1, :] + table[1:2, :] * 256 + table[2:3, :] * 65536 + (table[3:4, :] << 24)
    low, high = (jnp.broadcast_to(word[:, i * LANES : (i + 1) * LANES], (8, LANES)) for i in range(2))
    high_next = pltpu.roll(high, LANES - 1, 1)
    words[0] = low
    words[1] = high
    words[2] = jnp.where(small_lane == LANES - 1, high_next, pltpu.roll(low, LANES - 1, 1))
    words[3] = high_next
    lowest_first = jnp.broadcast_to(order[...], (8, LANES)) == 0
    first_half_front = lowest_first == near_half

    def second_stage(f, told=False):
        arrived(1, f, (2, 3, 4, 5))
        edges = edge_terms(1, f)

        def layers(d):
            centre, tend = tendency(1, f, edges, d)
            before = ext1[f, 4 + d : 4 + d + CHUNK, TOP : TOP + NR, :].reshape(ROWS, LANES)
            out[f, d : d + CHUNK] = (0.5 * (before + centre) + 0.1 * tend).reshape(CHUNK, NR, LANES)

        for d in range(CHUNK, ND - CHUNK, CHUNK):
            layers(d)
        arrived(1, f, (0, 1))
        if told:
            for side, peer in enumerate((beside("depth", 1), beside("depth", -1))):
                pl.semaphore_signal(token.at[side], inc=1, device_id=peer, device_id_type=MESH)
        for d in (0, ND - CHUNK):
            layers(d)

    second_stage(3, True)

    total = None
    for half in range(2):
        rest = out[3, half * 8 : half * 8 + 8].reshape(LANES, LANES)
        for piece in range(3):
            coarse = rest.astype(jnp.bfloat16)
            if piece < 2:
                rest = rest - coarse.astype(jnp.float32)
            term = jnp.dot(coarse, filters[half], preferred_element_type=jnp.float32)
            total = term if total is None else total + term
    texture[...] = total * 255.0

    def looked_up(sample):
        level = jnp.clip(sample, 0.0, 255.0)
        index = jnp.minimum(level.astype(jnp.int32), 254)
        fraction = level - index.astype(jnp.float32)
        place = index & (LANES - 1)
        upper_half = index >= LANES

        def pick(first):
            one = jnp.take_along_axis(words[first], place, axis=1, mode="promise_in_bounds")
            two = jnp.take_along_axis(words[first + 1], place, axis=1, mode="promise_in_bounds")
            return jnp.where(upper_half, two, one)

        def channels(value):
            spread = [value & 255, lax.shift_right_logical(value, 8) & 255, lax.shift_right_logical(value, 16) & 255,
                      lax.shift_right_logical(value, 24)]
            return [channel.astype(jnp.float32) for channel in spread]

        return channels(pick(0)), channels(pick(2)), fraction

    def peer_at(step):
        return lax.rem(my_depth + step, n_depth)

    def part_copy(step):
        peer = peer_at(step)
        return pltpu.make_async_remote_copy(
            src_ref=part.at[peer], dst_ref=mixed.at[my_depth], send_sem=part_send.at[step],
            recv_sem=part_recv.at[my_depth], device_id={"depth": peer}, device_id_type=MESH)

    def part_arrival(step):
        peer = peer_at(step)
        return pltpu.make_async_remote_copy(
            src_ref=part.at[peer], dst_ref=mixed.at[peer], send_sem=part_send.at[step],
            recv_sem=part_recv.at[peer], device_id={"depth": peer}, device_id_type=MESH)

    def final_copy(step):
        peer = peer_at(step)
        return pltpu.make_async_remote_copy(
            src_ref=final.at[my_depth], dst_ref=final.at[my_depth], send_sem=fin_send.at[step],
            recv_sem=fin_recv.at[my_depth], device_id={"depth": peer}, device_id_type=MESH)

    def final_arrival(step):
        peer = peer_at(step)
        return pltpu.make_async_remote_copy(
            src_ref=final.at[peer], dst_ref=final.at[peer], send_sem=fin_send.at[step],
            recv_sem=fin_recv.at[peer], device_id={"depth": peer}, device_id_type=MESH)

    def rendered(block):
        base = row_base(block)
        samples = []
        for pair in range(8):
            sample = None
            for i in range(4):
                term = weights[block, pair, i] * texture[pl.ds(pair * NR + base + i, 1), :]
                sample = term if sample is None else sample + term
            samples.append(sample)
        clear = jnp.ones((8, LANES), jnp.float32)
        sums = [jnp.zeros((8, LANES), jnp.float32) for _ in range(3)]
        for k in range(8):
            below, above, fraction = looked_up(jnp.where(lowest_first, samples[k], samples[7 - k]))
            alpha = (below[3] + (above[3] - below[3]) * fraction) * (6.0 / SLICES / 255.0)
            weight = clear * alpha
            share = weight * fraction
            keep = weight - share
            for c in range(3):
                sums[c] = sums[c] + (keep * below[c] + share * above[c])
            clear = clear - weight
        sums = [value * (1.0 / 255.0) for value in sums] + [1.0 - clear]
        turned = [pltpu.roll(value, PIX, 1) for value in sums]
        front_alpha = jnp.where(first_half_front, sums[3], turned[3])
        pieces = []
        for c in (0, 2):
            near = jnp.where(near_half, sums[c], turned[c + 1])
            far = jnp.where(near_half, turned[c], sums[c + 1])
            front = jnp.where(lowest_first, near, far)
            back = jnp.where(lowest_first, far, near)
            pieces.append(front + (1.0 - front_alpha) * back)
        return pieces

    for step in (4, 3, 5, 2, 6, 1, 7, 0):
        block = peer_at(step)
        pieces = rendered(block)
        for i in range(2):
            if step:
                part[block, i] = pieces[i]
            else:
                mixed[my_depth, i] = pieces[i]
        if step == 4:
            for side in range(2):
                pl.semaphore_wait(token.at[side], 1)
        if step:
            part_copy(step).start()

    columns_part(ext1, 2)
    first_stage(2)
    for f in FIELDS[1:3]:
        columns_part(ext2, f)
        second_stage(f)

    for step in range(1, n_depth):
        part_arrival(step).wait_recv()
    clear = jnp.ones((8, LANES), jnp.float32)
    sums = [jnp.zeros((8, LANES), jnp.float32) for _ in range(2)]
    for k in range(n_depth):
        pair = [jnp.where(lowest_first, mixed[k, i], mixed[n_depth - 1 - k, i]) for i in range(2)]
        alpha = jnp.where(near_half, pltpu.roll(pair[1], PIX, 1), pair[1])
        sums = [total + clear * value for total, value in zip(sums, pair)]
        clear = clear * (1.0 - alpha)
    for i in range(2):
        final[my_depth, i] = sums[i]
    for step in (4, 3, 5, 2, 6, 1, 7):
        final_copy(step).start()
    columns_part(ext2, 2)
    second_stage(2)
    for stage in range(2):
        for f in FIELDS:
            for copy in face_copies(stage, f) + column_copies(stage, f):
                copy.wait_send()
    for step in range(1, n_depth):
        part_copy(step).wait_send()
    for step in range(1, n_depth):
        final_arrival(step).wait_recv()
    for step in range(1, n_depth):
        final_copy(step).wait_send()


def finish(out, final, new_state, image, tile, sem, tile_sem):
    copies = [pltpu.make_async_copy(out.at[f], new_state.at[f], sem.at[f]) for f in range(4)]
    for copy in copies:
        copy.start()
    for block in range(8):
        for i in range(2):
            value = final[block, i]
            tile[2 * i, 8 * block : 8 * block + 8, :] = value[:, :PIX]
            tile[2 * i + 1, 8 * block : 8 * block + 8, :] = value[:, PIX:]
    copies.append(pltpu.make_async_copy(tile, image, tile_sem))
    copies[4].start()
    for copy in copies:
        copy.wait()


def solution(mesh):
    sizes = tuple(mesh.shape[axis] for axis in ("depth", "row", "col"))
    f32 = jnp.float32
    any_space = pl.BlockSpec(memory_space=pl.ANY)
    vmem = pl.BlockSpec(memory_space=pltpu.VMEM)
    extended = (4, ND + 8, NR + 16, LANES)

    def local(state, velocity, view_order, tf_table):
        held = pl.pallas_call(
            functools.partial(kernel, sizes),
            out_shape=(pltpu.VMEM((4, ND, NR, LANES), f32), pltpu.VMEM((8, 2, 8, LANES), f32)),
            in_specs=[any_space] * 4,
            out_specs=(vmem, vmem),
            scratch_shapes=[
                pltpu.VMEM(extended, f32),
                pltpu.VMEM(extended, f32),
                pltpu.VMEM((3, ND, NR, LANES), f32),
                pltpu.VMEM((2, ND, NR, LANES), f32),
                pltpu.VMEM((4, ND, NR, LANES), f32),
                pltpu.VMEM((2, 4, NR, LANES), f32),
                pltpu.VMEM((2, 2, 4, NR, LANES), f32),
                pltpu.VMEM((NR, LANES), f32),
                pltpu.VMEM((8, 8, 4, 8, LANES), f32),
                pltpu.VMEM((2, LANES, LANES), jnp.bfloat16),
                pltpu.VMEM((4, 8, LANES), jnp.int32),
                pltpu.VMEM((1, 1), jnp.int32),
                pltpu.VMEM((4, 2 * LANES), jnp.int32),
                pltpu.VMEM((LANES, LANES), f32),
                pltpu.VMEM((8, 2, 8, LANES), f32),
                pltpu.VMEM((8, 2, 8, LANES), f32),
                pltpu.SemaphoreType.DMA((4,)),
                pltpu.SemaphoreType.DMA,
                pltpu.SemaphoreType.DMA((2,)),
                pltpu.SemaphoreType.DMA((2, 4, 6)),
                pltpu.SemaphoreType.DMA((2, 4, 6)),
                pltpu.SemaphoreType.DMA((8,)),
                pltpu.SemaphoreType.DMA((8,)),
                pltpu.SemaphoreType.DMA((8,)),
                pltpu.SemaphoreType.DMA((8,)),
                pltpu.SemaphoreType.REGULAR((2,)),
            ],
            compiler_params=pltpu.CompilerParams(collective_id=0, has_side_effects=True),
        )(state, velocity, view_order, tf_table)
        return tuple(pl.pallas_call(
            finish,
            out_shape=(
                jax.ShapeDtypeStruct((4, ND, NR, LANES), f32),
                jax.ShapeDtypeStruct((4, PIX, PIX), f32),
            ),
            in_specs=[vmem, vmem],
            out_specs=(any_space, any_space),
            scratch_shapes=[pltpu.VMEM((4, PIX, PIX), f32), pltpu.SemaphoreType.DMA((4,)), pltpu.SemaphoreType.DMA],
        )(*(pltpu.with_memory_space_constraint(value, pltpu.VMEM) for value in held)))

    return jax.shard_map(
        local,
        mesh=mesh,
        in_specs=(P(None, "depth", "row", "col"), P(None, "depth", "row", "col"), P("row", "col"), P()),
        out_specs=(P(None, "depth", "row", "col"), P(None, "row", "col")),
        check_vma=False,
    )
```

```python
import functools

import jax
import jax.numpy as jnp
from jax import lax
from jax.experimental import pallas as pl
from jax.experimental.pallas import tpu as pltpu
from jax.sharding import PartitionSpec as P

MESH = pl.DeviceIdType.MESH
FIRST_COEF = (0.8, -0.2, 4.0 / 105.0, -1.0 / 280.0)
SECOND_COEF = (1.6, -0.2, 8.0 / 315.0, -1.0 / 560.0)
CENTER_COEF = -205.0 / 72.0
DIFFUSIVITY = (0.05, 0.04, 0.03, 0.08)
SOURCE = (-1.0, -1.5, 2.5, 0.8)
FIELDS = (3, 0, 1, 2)
ND = 16
NR = 16
LANES = 128
TOP = 8
CHUNK = 4
ROWS = CHUNK * NR
SLICES = 128
PIX = 64


def kernel(sizes, state, velocity, order_in, table_in, out, final, ext1, ext2, vel, rate, partial, pack, got,
           flow_pack, weights, filters, words, order, table, texture, part, mixed, in_sem, vel_sem, small_sem,
           send_sem, recv_sem, part_send, part_recv, fin_send, fin_recv, token):
    n_depth, n_row, n_col = sizes
    my_depth, my_row, my_col = lax.axis_index("depth"), lax.axis_index("row"), lax.axis_index("col")
    places = {"depth": (my_depth, n_depth), "row": (my_row, n_row), "col": (my_col, n_col)}

    def beside(axis, step):
        at, count = places[axis]
        return {axis: lax.rem(at + step + count, count)}

    barrier = pltpu.get_barrier_semaphore()
    neighbours = [beside(axis, step) for axis in ("depth", "row", "col") for step in (1, -1)]
    for peer in neighbours:
        pl.semaphore_signal(barrier, inc=1, device_id=peer, device_id_type=MESH)

    def load_field(f):
        return pltpu.make_async_copy(state.at[f], ext1.at[f, 4 : 4 + ND, TOP : TOP + NR, :], in_sem.at[f])

    load_velocity = pltpu.make_async_copy(velocity, vel, vel_sem)
    load_order = pltpu.make_async_copy(order_in, order, small_sem.at[0])
    load_table = pltpu.make_async_copy(table_in, table, small_sem.at[1])
    for f in FIELDS:
        load_field(f).start()
    load_velocity.start()
    load_order.start()
    load_table.start()

    lane = lax.broadcasted_iota(jnp.int32, (NR, LANES), 1)
    chunk_lane = lax.broadcasted_iota(jnp.int32, (ROWS, LANES), 1)
    chunk_edge = (chunk_lane < 4) | (chunk_lane >= LANES - 4)
    small_lane = lax.broadcasted_iota(jnp.int32, (8, LANES), 1)
    sub = lax.broadcasted_iota(jnp.int32, (8, LANES), 0)
    near_half = small_lane < PIX
    in_group = lane & 7
    low_side = in_group < 4

    def row_base(block):
        return jnp.clip(2 * block - 2 + (2 * my_depth + 5) // 8, 0, NR - 4)

    def remote(stage, f, index, source, target, peer):
        return pltpu.make_async_remote_copy(
            src_ref=source, dst_ref=target, send_sem=send_sem.at[stage, f, index],
            recv_sem=recv_sem.at[stage, f, index], device_id=peer, device_id_type=MESH)

    def face_copies(stage, f):
        if stage == 0:
            source, target, d0, r0 = state, ext1, 0, 0
        else:
            source, target, d0, r0 = ext2, ext2, 4, TOP
        rows, layers = pl.ds(r0, NR), pl.ds(d0, ND)
        return [
            remote(stage, f, 0, source.at[f, pl.ds(d0 + ND - 4, 4), rows, :],
                   target.at[f, 0:4, TOP : TOP + NR, :], beside("depth", 1)),
            remote(stage, f, 1, source.at[f, pl.ds(d0, 4), rows, :],
                   target.at[f, 4 + ND : 8 + ND, TOP : TOP + NR, :], beside("depth", -1)),
            remote(stage, f, 2, source.at[f, layers, pl.ds(r0 + NR - 4, 4), :],
                   target.at[f, 4 : 4 + ND, TOP - 4 : TOP, :], beside("row", 1)),
            remote(stage, f, 3, source.at[f, layers, pl.ds(r0, 4), :],
                   target.at[f, 4 : 4 + ND, TOP + NR : TOP + NR + 4, :], beside("row", -1)),
        ]

    def column_copies(stage, f):
        return [
            remote(stage, f, 4, pack.at[stage, f], got.at[stage, 0, f], beside("col", 1)),
            remote(stage, f, 5, pack.at[stage, f], got.at[stage, 1, f], beside("col", -1)),
        ]

    lane_group = lane // 8

    def packed(layers):
        gathered = None
        for d, values in enumerate(layers):
            turned = pltpu.roll(values, (4 + 8 * d) % LANES, 1)
            gathered = turned if d == 0 else jnp.where(lane_group == d, turned, gathered)
        return gathered

    def body(ext, f, d):
        return ext[f, 4 + d, TOP : TOP + NR, :]

    pl.semaphore_wait(barrier, len(neighbours))
    def rates(ext, stage):
        for d in range(0, ND, CHUNK):
            v0, v1, v3 = (ext[f, 4 + d : 4 + d + CHUNK, TOP : TOP + NR, :] for f in (0, 1, 3))
            rate[stage, d : d + CHUNK] = 2.0 * v0 * v1 * jax.nn.sigmoid(8.0 * (v3 - 0.5))

    def flow(spatial, d):
        return vel[spatial, d : d + CHUNK].reshape(ROWS, LANES)

    def columns_part(ext, f):
        for d in range(0, ND, CHUNK):
            centre = ext[f, 4 + d : 4 + d + CHUNK, TOP : TOP + NR, :].reshape(ROWS, LANES)
            total = (3.0 * CENTER_COEF * DIFFUSIVITY[f]) * centre
            gradient = None
            for offset in range(1, 5):
                ahead, behind = pltpu.roll(centre, LANES - offset, 1), pltpu.roll(centre, offset, 1)
                term = FIRST_COEF[offset - 1] * (ahead - behind)
                gradient = term if gradient is None else gradient + term
                total = total + (SECOND_COEF[offset - 1] * DIFFUSIVITY[f]) * (ahead + behind)
            partial[f, d : d + CHUNK] = (total - flow(2, d) * gradient).reshape(CHUNK, NR, LANES)

    def edge_terms(stage, f):
        change = jnp.where(low_side, got[stage, 0, f], got[stage, 1, f]) - pack[stage, f]
        second = first = None
        for offset in range(1, 5):
            ahead, behind = pltpu.roll(change, LANES - offset, 1), pltpu.roll(change, offset, 1)
            reach = (low_side & (in_group + offset >= 4)) | ((in_group >= 4) & (in_group - offset <= 3))
            moved = jnp.where(reach, jnp.where(low_side, ahead, behind), 0.0)
            one, two = FIRST_COEF[offset - 1] * moved, (SECOND_COEF[offset - 1] * DIFFUSIVITY[f]) * moved
            first = one if first is None else first + one
            second = two if second is None else second + two
        first = jnp.where(low_side, first, -first)
        return second - flow_pack[...] * first

    def tendency(stage, f, edges, d):
        ext = (ext1, ext2)[stage]

        def window(depth_shift, row_shift):
            d0, r0 = d + 4 + depth_shift, TOP + row_shift
            return ext[f, d0 : d0 + CHUNK, r0 : r0 + NR, :].reshape(ROWS, LANES)

        total = partial[f, d : d + CHUNK].reshape(ROWS, LANES)
        total = total + SOURCE[f] * rate[stage, d : d + CHUNK].reshape(ROWS, LANES)
        along_depth = along_rows = None
        for offset in range(1, 5):
            up, down = window(offset, 0), window(-offset, 0)
            ahead, behind = window(0, offset), window(0, -offset)
            total = total + (SECOND_COEF[offset - 1] * DIFFUSIVITY[f]) * ((up + down) + (ahead + behind))
            one, two = FIRST_COEF[offset - 1] * (up - down), FIRST_COEF[offset - 1] * (ahead - behind)
            along_depth = one if along_depth is None else along_depth + one
            along_rows = two if along_rows is None else along_rows + two
        total = total - (flow(0, d) * along_depth + flow(1, d) * along_rows)
        edge = jnp.concatenate([pltpu.roll(edges, (124 - 8 * (d + i)) % LANES, 1) for i in range(CHUNK)], 0)
        return window(0, 0), total + jnp.where(chunk_edge, edge, 0.0)

    def arrived(stage, f, indices):
        copies = face_copies(stage, f) + column_copies(stage, f)
        for index in indices:
            copies[index].wait_recv()

    def prepare():
        far_slice = 8 * (small_lane // PIX)
        for block in range(8):
            base = row_base(block)
            row = (8 * block + sub).astype(jnp.float32)
            slice_at = (16 * my_depth + far_slice).astype(jnp.float32)
            first_spot = (row + 0.5) * 0.25 - 0.5 + 2.0 * ((slice_at + 0.5) / SLICES - 0.5)
            for pair in range(8):
                spot = jnp.clip(first_spot + pair * (2.0 / SLICES), 0.0, NR - 1.0) - base.astype(jnp.float32)
                for i in range(4):
                    weights[block, pair, i] = jnp.maximum(0.0, 1.0 - jnp.abs(spot - float(i)))
        from_column = lax.broadcasted_iota(jnp.int32, (LANES, LANES), 0).astype(jnp.float32)
        to_lane = lax.broadcasted_iota(jnp.int32, (LANES, LANES), 1)
        to_column = (to_lane & (PIX - 1)).astype(jnp.float32)
        spot = jnp.clip((to_column + 0.5) * 2.0 - 0.5, 0.0, LANES - 1.0)
        filter_all = jnp.maximum(0.0, 1.0 - jnp.abs(spot - from_column) / 2.0) / 2.0
        for half in range(2):
            filters[half] = jnp.where(to_lane // PIX == half, filter_all, 0.0).astype(jnp.bfloat16)

    def send_first(f):
        for copy in face_copies(0, f):
            copy.start()
        if f > 1:
            load_field(f).wait()
        pack[0, f] = packed([body(ext1, f, d) for d in range(ND)])
        for copy in column_copies(0, f):
            copy.start()

    send_first(3)
    load_velocity.wait()
    flow_pack[...] = packed([vel[2, d] for d in range(ND)])
    columns_part(ext1, 3)
    load_field(0).wait()
    send_first(0)
    columns_part(ext1, 0)
    load_field(1).wait()
    send_first(1)
    rates(ext1, 0)
    columns_part(ext1, 1)
    prepare()

    def first_stage(f):
        arrived(0, f, (2, 3, 4, 5))
        edges = edge_terms(0, f)

        def layers(d):
            centre, tend = tendency(0, f, edges, d)
            ext2[f, 4 + d : 4 + d + CHUNK, TOP : TOP + NR, :] = (centre + 0.2 * tend).reshape(CHUNK, NR, LANES)

        copies = face_copies(1, f)
        for d in range(CHUNK, ND - CHUNK, CHUNK):
            layers(d)
        arrived(0, f, (0, 1))
        layers(0)
        copies[1].start()
        layers(ND - CHUNK)
        for index in (0, 2, 3):
            copies[index].start()
        pack[1, f] = packed([body(ext2, f, d) for d in range(ND)])
        for copy in column_copies(1, f):
            copy.start()

    first_stage(3)
    first_stage(0)
    first_stage(1)
    send_first(2)
    columns_part(ext2, 3)
    rates(ext2, 1)

    load_order.wait()
    load_table.wait()
    word = table[0:1, :] + table[1:2, :] * 256 + table[2:3, :] * 65536 + (table[3:4, :] << 24)
    low, high = (jnp.broadcast_to(word[:, i * LANES : (i + 1) * LANES], (8, LANES)) for i in range(2))
    high_next = pltpu.roll(high, LANES - 1, 1)
    words[0] = low
    words[1] = high
    words[2] = jnp.where(small_lane == LANES - 1, high_next, pltpu.roll(low, LANES - 1, 1))
    words[3] = high_next
    lowest_first = jnp.broadcast_to(order[...], (8, LANES)) == 0
    first_half_front = lowest_first == near_half

    def second_stage(f, told=False):
        arrived(1, f, (2, 3, 4, 5))
        edges = edge_terms(1, f)

        def layers(d):
            centre, tend = tendency(1, f, edges, d)
            before = ext1[f, 4 + d : 4 + d + CHUNK, TOP : TOP + NR, :].reshape(ROWS, LANES)
            out[f, d : d + CHUNK] = (0.5 * (before + centre) + 0.1 * tend).reshape(CHUNK, NR, LANES)

        for d in range(CHUNK, ND - CHUNK, CHUNK):
            layers(d)
        arrived(1, f, (0, 1))
        if told:
            for side, peer in enumerate((beside("depth", 1), beside("depth", -1))):
                pl.semaphore_signal(token.at[side], inc=1, device_id=peer, device_id_type=MESH)
        for d in (0, ND - CHUNK):
            layers(d)

    second_stage(3, True)

    total = None
    for half in range(2):
        rest = out[3, half * 8 : half * 8 + 8].reshape(LANES, LANES)
        for piece in range(3):
            coarse = rest.astype(jnp.bfloat16)
            if piece < 2:
                rest = rest - coarse.astype(jnp.float32)
            term = jnp.dot(coarse, filters[half], preferred_element_type=jnp.float32)
            total = term if total is None else total + term
    texture[...] = total * 255.0

    def looked_up(sample):
        level = jnp.clip(sample, 0.0, 255.0)
        index = jnp.minimum(level.astype(jnp.int32), 254)
        fraction = level - index.astype(jnp.float32)
        place = index & (LANES - 1)
        upper_half = index >= LANES

        def pick(first):
            one = jnp.take_along_axis(words[first], place, axis=1, mode="promise_in_bounds")
            two = jnp.take_along_axis(words[first + 1], place, axis=1, mode="promise_in_bounds")
            return jnp.where(upper_half, two, one)

        def channels(value):
            spread = [value & 255, lax.shift_right_logical(value, 8) & 255, lax.shift_right_logical(value, 16) & 255,
                      lax.shift_right_logical(value, 24)]
            return [channel.astype(jnp.float32) for channel in spread]

        return channels(pick(0)), channels(pick(2)), fraction

    def peer_at(step):
        return lax.rem(my_depth + step, n_depth)

    def part_copy(step):
        peer = peer_at(step)
        return pltpu.make_async_remote_copy(
            src_ref=part.at[peer], dst_ref=mixed.at[my_depth], send_sem=part_send.at[step],
            recv_sem=part_recv.at[my_depth], device_id={"depth": peer}, device_id_type=MESH)

    def part_arrival(step):
        peer = peer_at(step)
        return pltpu.make_async_remote_copy(
            src_ref=part.at[peer], dst_ref=mixed.at[peer], send_sem=part_send.at[step],
            recv_sem=part_recv.at[peer], device_id={"depth": peer}, device_id_type=MESH)

    def final_copy(step):
        peer = peer_at(step)
        return pltpu.make_async_remote_copy(
            src_ref=final.at[my_depth], dst_ref=final.at[my_depth], send_sem=fin_send.at[step],
            recv_sem=fin_recv.at[my_depth], device_id={"depth": peer}, device_id_type=MESH)

    def final_arrival(step):
        peer = peer_at(step)
        return pltpu.make_async_remote_copy(
            src_ref=final.at[peer], dst_ref=final.at[peer], send_sem=fin_send.at[step],
            recv_sem=fin_recv.at[peer], device_id={"depth": peer}, device_id_type=MESH)

    def rendered(block):
        base = row_base(block)
        samples = []
        for pair in range(8):
            sample = None
            for i in range(4):
                term = weights[block, pair, i] * texture[pl.ds(pair * NR + base + i, 1), :]
                sample = term if sample is None else sample + term
            samples.append(sample)
        clear = jnp.ones((8, LANES), jnp.float32)
        sums = [jnp.zeros((8, LANES), jnp.float32) for _ in range(3)]
        for k in range(8):
            below, above, fraction = looked_up(jnp.where(lowest_first, samples[k], samples[7 - k]))
            alpha = (below[3] + (above[3] - below[3]) * fraction) * (6.0 / SLICES / 255.0)
            weight = clear * alpha
            share = weight * fraction
            keep = weight - share
            for c in range(3):
                sums[c] = sums[c] + (keep * below[c] + share * above[c])
            clear = clear - weight
        sums = [value * (1.0 / 255.0) for value in sums] + [1.0 - clear]
        turned = [pltpu.roll(value, PIX, 1) for value in sums]
        front_alpha = jnp.where(first_half_front, sums[3], turned[3])
        pieces = []
        for c in (0, 2):
            near = jnp.where(near_half, sums[c], turned[c + 1])
            far = jnp.where(near_half, turned[c], sums[c + 1])
            front = jnp.where(lowest_first, near, far)
            back = jnp.where(lowest_first, far, near)
            pieces.append(front + (1.0 - front_alpha) * back)
        return pieces

    for steps in ((4,), (3, 5), (2, 6), (1, 7, 0)):
        for step in steps:
            block = peer_at(step)
            pieces = rendered(block)
            for i in range(2):
                if step:
                    part[block, i] = pieces[i]
                else:
                    mixed[my_depth, i] = pieces[i]
        if steps[0] == 4:
            for side in range(2):
                pl.semaphore_wait(token.at[side], 1)
        for step in steps:
            if step:
                part_copy(step).start()

    columns_part(ext1, 2)
    first_stage(2)
    for f in FIELDS[1:3]:
        columns_part(ext2, f)
        second_stage(f)

    for step in range(1, n_depth):
        part_arrival(step).wait_recv()
    clear = jnp.ones((8, LANES), jnp.float32)
    sums = [jnp.zeros((8, LANES), jnp.float32) for _ in range(2)]
    for k in range(n_depth):
        pair = [jnp.where(lowest_first, mixed[k, i], mixed[n_depth - 1 - k, i]) for i in range(2)]
        alpha = jnp.where(near_half, pltpu.roll(pair[1], PIX, 1), pair[1])
        sums = [total + clear * value for total, value in zip(sums, pair)]
        clear = clear * (1.0 - alpha)
    for i in range(2):
        final[my_depth, i] = sums[i]
    for step in (4, 3, 5, 2, 6, 1, 7):
        final_copy(step).start()
    columns_part(ext2, 2)
    second_stage(2)
    for stage in range(2):
        for f in FIELDS:
            for copy in face_copies(stage, f) + column_copies(stage, f):
                copy.wait_send()
    for step in range(1, n_depth):
        part_copy(step).wait_send()
    for step in range(1, n_depth):
        final_arrival(step).wait_recv()
    for step in range(1, n_depth):
        final_copy(step).wait_send()


def finish(out, final, new_state, image, tile, sem, tile_sem):
    copies = [pltpu.make_async_copy(out.at[f], new_state.at[f], sem.at[f]) for f in range(4)]
    for copy in copies:
        copy.start()
    for block in range(8):
        for i in range(2):
            value = final[block, i]
            tile[2 * i, 8 * block : 8 * block + 8, :] = value[:, :PIX]
            tile[2 * i + 1, 8 * block : 8 * block + 8, :] = value[:, PIX:]
    copies.append(pltpu.make_async_copy(tile, image, tile_sem))
    copies[4].start()
    for copy in copies:
        copy.wait()


def solution(mesh):
    sizes = tuple(mesh.shape[axis] for axis in ("depth", "row", "col"))
    f32 = jnp.float32
    any_space = pl.BlockSpec(memory_space=pl.ANY)
    hbm = pl.BlockSpec(memory_space=pltpu.HBM)
    vmem = pl.BlockSpec(memory_space=pltpu.VMEM)
    extended = (4, ND + 8, NR + 16, LANES)

    def local(state, velocity, view_order, tf_table):
        held = pl.pallas_call(
            functools.partial(kernel, sizes),
            out_shape=(pltpu.VMEM((4, ND, NR, LANES), f32), pltpu.VMEM((8, 2, 8, LANES), f32)),
            in_specs=[any_space, any_space, hbm, hbm],
            out_specs=(vmem, vmem),
            scratch_shapes=[
                pltpu.VMEM(extended, f32),
                pltpu.VMEM(extended, f32),
                pltpu.VMEM((3, ND, NR, LANES), f32),
                pltpu.VMEM((2, ND, NR, LANES), f32),
                pltpu.VMEM((4, ND, NR, LANES), f32),
                pltpu.VMEM((2, 4, NR, LANES), f32),
                pltpu.VMEM((2, 2, 4, NR, LANES), f32),
                pltpu.VMEM((NR, LANES), f32),
                pltpu.VMEM((8, 8, 4, 8, LANES), f32),
                pltpu.VMEM((2, LANES, LANES), jnp.bfloat16),
                pltpu.VMEM((4, 8, LANES), jnp.int32),
                pltpu.VMEM((1, 1), jnp.int32),
                pltpu.VMEM((4, 2 * LANES), jnp.int32),
                pltpu.VMEM((LANES, LANES), f32),
                pltpu.VMEM((8, 2, 8, LANES), f32),
                pltpu.VMEM((8, 2, 8, LANES), f32),
                pltpu.SemaphoreType.DMA((4,)),
                pltpu.SemaphoreType.DMA,
                pltpu.SemaphoreType.DMA((2,)),
                pltpu.SemaphoreType.DMA((2, 4, 6)),
                pltpu.SemaphoreType.DMA((2, 4, 6)),
                pltpu.SemaphoreType.DMA((8,)),
                pltpu.SemaphoreType.DMA((8,)),
                pltpu.SemaphoreType.DMA((8,)),
                pltpu.SemaphoreType.DMA((8,)),
                pltpu.SemaphoreType.REGULAR((2,)),
            ],
            compiler_params=pltpu.CompilerParams(collective_id=0, has_side_effects=True),
        )(state, velocity, view_order, tf_table)
        return tuple(pl.pallas_call(
            finish,
            out_shape=(
                jax.ShapeDtypeStruct((4, ND, NR, LANES), f32),
                jax.ShapeDtypeStruct((4, PIX, PIX), f32),
            ),
            in_specs=[vmem, vmem],
            out_specs=(any_space, any_space),
            scratch_shapes=[pltpu.VMEM((4, PIX, PIX), f32), pltpu.SemaphoreType.DMA((4,)), pltpu.SemaphoreType.DMA],
        )(*(pltpu.with_memory_space_constraint(value, pltpu.VMEM) for value in held)))

    return jax.shard_map(
        local,
        mesh=mesh,
        in_specs=(P(None, "depth", "row", "col"), P(None, "depth", "row", "col"), P("row", "col"), P()),
        out_specs=(P(None, "depth", "row", "col"), P(None, "row", "col")),
        check_vma=False,
    )
```

```python
import functools

import jax
import jax.numpy as jnp
from jax import lax
from jax.experimental import pallas as pl
from jax.experimental.pallas import tpu as pltpu
from jax.sharding import PartitionSpec as P

MESH = pl.DeviceIdType.MESH
FIRST_COEF = (0.8, -0.2, 4.0 / 105.0, -1.0 / 280.0)
SECOND_COEF = (1.6, -0.2, 8.0 / 315.0, -1.0 / 560.0)
CENTER_COEF = -205.0 / 72.0
DIFFUSIVITY = (0.05, 0.04, 0.03, 0.08)
SOURCE = (-1.0, -1.5, 2.5, 0.8)
FIELDS = (3, 0, 1, 2)
ND = 16
NR = 16
LANES = 128
TOP = 8
CHUNK = 4
ROWS = CHUNK * NR
SLICES = 128
PIX = 64


def kernel(sizes, state, velocity, order_in, table_in, out, final, ext1, ext2, vel, rate, partial, pack, got,
           flow_pack, weights, filters, words, order, table, texture, part, mixed, in_sem, vel_sem, small_sem,
           send_sem, recv_sem, part_send, part_recv, fin_send, fin_recv, token):
    n_depth, n_row, n_col = sizes
    my_depth, my_row, my_col = lax.axis_index("depth"), lax.axis_index("row"), lax.axis_index("col")
    places = {"depth": (my_depth, n_depth), "row": (my_row, n_row), "col": (my_col, n_col)}

    def beside(axis, step):
        at, count = places[axis]
        return {axis: lax.rem(at + step + count, count)}

    barrier = pltpu.get_barrier_semaphore()
    neighbours = [beside(axis, step) for axis in ("depth", "row", "col") for step in (1, -1)]
    for peer in neighbours:
        pl.semaphore_signal(barrier, inc=1, device_id=peer, device_id_type=MESH)

    def load_field(f):
        return pltpu.make_async_copy(state.at[f], ext1.at[f, 4 : 4 + ND, TOP : TOP + NR, :], in_sem.at[f])

    load_velocity = pltpu.make_async_copy(velocity, vel, vel_sem)
    load_order = pltpu.make_async_copy(order_in, order, small_sem.at[0])
    load_table = pltpu.make_async_copy(table_in, table, small_sem.at[1])
    for f in FIELDS:
        load_field(f).start()
    load_velocity.start()
    load_order.start()
    load_table.start()

    lane = lax.broadcasted_iota(jnp.int32, (NR, LANES), 1)
    chunk_lane = lax.broadcasted_iota(jnp.int32, (ROWS, LANES), 1)
    chunk_edge = (chunk_lane < 4) | (chunk_lane >= LANES - 4)
    small_lane = lax.broadcasted_iota(jnp.int32, (8, LANES), 1)
    sub = lax.broadcasted_iota(jnp.int32, (8, LANES), 0)
    near_half = small_lane < PIX
    in_group = lane & 7
    low_side = in_group < 4

    def row_base(block):
        return jnp.clip(2 * block - 2 + (2 * my_depth + 5) // 8, 0, NR - 4)

    def remote(stage, f, index, source, target, peer):
        return pltpu.make_async_remote_copy(
            src_ref=source, dst_ref=target, send_sem=send_sem.at[stage, f, index],
            recv_sem=recv_sem.at[stage, f, index], device_id=peer, device_id_type=MESH)

    def face_copies(stage, f):
        if stage == 0:
            source, target, d0, r0 = state, ext1, 0, 0
        else:
            source, target, d0, r0 = ext2, ext2, 4, TOP
        rows, layers = pl.ds(r0, NR), pl.ds(d0, ND)
        return [
            remote(stage, f, 0, source.at[f, pl.ds(d0 + ND - 4, 4), rows, :],
                   target.at[f, 0:4, TOP : TOP + NR, :], beside("depth", 1)),
            remote(stage, f, 1, source.at[f, pl.ds(d0, 4), rows, :],
                   target.at[f, 4 + ND : 8 + ND, TOP : TOP + NR, :], beside("depth", -1)),
            remote(stage, f, 2, source.at[f, layers, pl.ds(r0 + NR - 4, 4), :],
                   target.at[f, 4 : 4 + ND, TOP - 4 : TOP, :], beside("row", 1)),
            remote(stage, f, 3, source.at[f, layers, pl.ds(r0, 4), :],
                   target.at[f, 4 : 4 + ND, TOP + NR : TOP + NR + 4, :], beside("row", -1)),
        ]

    def column_copies(stage, f):
        return [
            remote(stage, f, 4, pack.at[stage, f], got.at[stage, 0, f], beside("col", 1)),
            remote(stage, f, 5, pack.at[stage, f], got.at[stage, 1, f], beside("col", -1)),
        ]

    lane_group = lane // 8

    def packed(layers):
        gathered = None
        for d, values in enumerate(layers):
            turned = pltpu.roll(values, (4 + 8 * d) % LANES, 1)
            gathered = turned if d == 0 else jnp.where(lane_group == d, turned, gathered)
        return gathered

    def body(ext, f, d):
        return ext[f, 4 + d, TOP : TOP + NR, :]

    pl.semaphore_wait(barrier, len(neighbours))
    def rates(ext, stage):
        for d in range(0, ND, CHUNK):
            v0, v1, v3 = (ext[f, 4 + d : 4 + d + CHUNK, TOP : TOP + NR, :] for f in (0, 1, 3))
            rate[stage, d : d + CHUNK] = 2.0 * v0 * v1 * jax.nn.sigmoid(8.0 * (v3 - 0.5))

    def flow(spatial, d):
        return vel[spatial, d : d + CHUNK].reshape(ROWS, LANES)

    def columns_part(ext, f):
        for d in range(0, ND, CHUNK):
            centre = ext[f, 4 + d : 4 + d + CHUNK, TOP : TOP + NR, :].reshape(ROWS, LANES)
            total = (3.0 * CENTER_COEF * DIFFUSIVITY[f]) * centre
            gradient = None
            for offset in range(1, 5):
                ahead, behind = pltpu.roll(centre, LANES - offset, 1), pltpu.roll(centre, offset, 1)
                term = FIRST_COEF[offset - 1] * (ahead - behind)
                gradient = term if gradient is None else gradient + term
                total = total + (SECOND_COEF[offset - 1] * DIFFUSIVITY[f]) * (ahead + behind)
            partial[f, d : d + CHUNK] = (total - flow(2, d) * gradient).reshape(CHUNK, NR, LANES)

    def edge_terms(stage, f):
        change = jnp.where(low_side, got[stage, 0, f], got[stage, 1, f]) - pack[stage, f]
        second = first = None
        for offset in range(1, 5):
            ahead, behind = pltpu.roll(change, LANES - offset, 1), pltpu.roll(change, offset, 1)
            reach = (low_side & (in_group + offset >= 4)) | ((in_group >= 4) & (in_group - offset <= 3))
            moved = jnp.where(reach, jnp.where(low_side, ahead, behind), 0.0)
            one, two = FIRST_COEF[offset - 1] * moved, (SECOND_COEF[offset - 1] * DIFFUSIVITY[f]) * moved
            first = one if first is None else first + one
            second = two if second is None else second + two
        first = jnp.where(low_side, first, -first)
        return second - flow_pack[...] * first

    def tendency(stage, f, edges, d):
        ext = (ext1, ext2)[stage]

        def window(depth_shift, row_shift):
            d0, r0 = d + 4 + depth_shift, TOP + row_shift
            return ext[f, d0 : d0 + CHUNK, r0 : r0 + NR, :].reshape(ROWS, LANES)

        total = partial[f, d : d + CHUNK].reshape(ROWS, LANES)
        total = total + SOURCE[f] * rate[stage, d : d + CHUNK].reshape(ROWS, LANES)
        along_depth = along_rows = None
        for offset in range(1, 5):
            up, down = window(offset, 0), window(-offset, 0)
            ahead, behind = window(0, offset), window(0, -offset)
            total = total + (SECOND_COEF[offset - 1] * DIFFUSIVITY[f]) * ((up + down) + (ahead + behind))
            one, two = FIRST_COEF[offset - 1] * (up - down), FIRST_COEF[offset - 1] * (ahead - behind)
            along_depth = one if along_depth is None else along_depth + one
            along_rows = two if along_rows is None else along_rows + two
        total = total - (flow(0, d) * along_depth + flow(1, d) * along_rows)
        edge = jnp.concatenate([pltpu.roll(edges, (124 - 8 * (d + i)) % LANES, 1) for i in range(CHUNK)], 0)
        return window(0, 0), total + jnp.where(chunk_edge, edge, 0.0)

    def arrived(stage, f, indices):
        copies = face_copies(stage, f) + column_copies(stage, f)
        for index in indices:
            copies[index].wait_recv()

    def prepare():
        far_slice = 8 * (small_lane // PIX)
        for block in range(8):
            base = row_base(block)
            row = (8 * block + sub).astype(jnp.float32)
            slice_at = (16 * my_depth + far_slice).astype(jnp.float32)
            first_spot = (row + 0.5) * 0.25 - 0.5 + 2.0 * ((slice_at + 0.5) / SLICES - 0.5)
            for pair in range(8):
                spot = jnp.clip(first_spot + pair * (2.0 / SLICES), 0.0, NR - 1.0) - base.astype(jnp.float32)
                for i in range(4):
                    weights[block, pair, i] = jnp.maximum(0.0, 1.0 - jnp.abs(spot - float(i)))
        from_column = lax.broadcasted_iota(jnp.int32, (LANES, LANES), 0).astype(jnp.float32)
        to_lane = lax.broadcasted_iota(jnp.int32, (LANES, LANES), 1)
        to_column = (to_lane & (PIX - 1)).astype(jnp.float32)
        spot = jnp.clip((to_column + 0.5) * 2.0 - 0.5, 0.0, LANES - 1.0)
        filter_all = jnp.maximum(0.0, 1.0 - jnp.abs(spot - from_column) / 2.0) / 2.0
        for half in range(2):
            filters[half] = jnp.where(to_lane // PIX == half, filter_all, 0.0).astype(jnp.bfloat16)

    def send_first(f):
        for copy in face_copies(0, f):
            copy.start()
        if f > 1:
            load_field(f).wait()
        pack[0, f] = packed([body(ext1, f, d) for d in range(ND)])
        for copy in column_copies(0, f):
            copy.start()

    send_first(3)
    load_velocity.wait()
    flow_pack[...] = packed([vel[2, d] for d in range(ND)])
    columns_part(ext1, 3)
    load_field(0).wait()
    send_first(0)
    columns_part(ext1, 0)
    load_field(1).wait()
    send_first(1)
    rates(ext1, 0)
    columns_part(ext1, 1)
    prepare()

    def first_stage(f):
        arrived(0, f, (2, 3, 4, 5))
        edges = edge_terms(0, f)

        def layers(d):
            centre, tend = tendency(0, f, edges, d)
            ext2[f, 4 + d : 4 + d + CHUNK, TOP : TOP + NR, :] = (centre + 0.2 * tend).reshape(CHUNK, NR, LANES)

        copies = face_copies(1, f)
        for d in range(CHUNK, ND - CHUNK, CHUNK):
            layers(d)
        arrived(0, f, (0, 1))
        layers(0)
        copies[1].start()
        layers(ND - CHUNK)
        for index in (0, 2, 3):
            copies[index].start()
        pack[1, f] = packed([body(ext2, f, d) for d in range(ND)])
        for copy in column_copies(1, f):
            copy.start()

    first_stage(3)
    first_stage(0)
    first_stage(1)
    send_first(2)
    columns_part(ext2, 3)
    rates(ext2, 1)

    load_order.wait()
    load_table.wait()
    word = table[0:1, :] + table[1:2, :] * 256 + table[2:3, :] * 65536 + (table[3:4, :] << 24)
    low, high = (jnp.broadcast_to(word[:, i * LANES : (i + 1) * LANES], (8, LANES)) for i in range(2))
    high_next = pltpu.roll(high, LANES - 1, 1)
    words[0] = low
    words[1] = high
    words[2] = jnp.where(small_lane == LANES - 1, high_next, pltpu.roll(low, LANES - 1, 1))
    words[3] = high_next
    lowest_first = jnp.broadcast_to(order[...], (8, LANES)) == 0
    first_half_front = lowest_first == near_half

    def second_stage(f, told=False):
        arrived(1, f, (2, 3, 4, 5))
        edges = edge_terms(1, f)

        def layers(d):
            centre, tend = tendency(1, f, edges, d)
            before = ext1[f, 4 + d : 4 + d + CHUNK, TOP : TOP + NR, :].reshape(ROWS, LANES)
            out[f, d : d + CHUNK] = (0.5 * (before + centre) + 0.1 * tend).reshape(CHUNK, NR, LANES)

        for d in range(CHUNK, ND - CHUNK, CHUNK):
            layers(d)
        arrived(1, f, (0, 1))
        if told:
            for side, peer in enumerate((beside("depth", 1), beside("depth", -1))):
                pl.semaphore_signal(token.at[side], inc=1, device_id=peer, device_id_type=MESH)
        for d in (0, ND - CHUNK):
            layers(d)

    second_stage(3, True)

    total = None
    for half in range(2):
        rest = out[3, half * 8 : half * 8 + 8].reshape(LANES, LANES)
        for piece in range(3):
            coarse = rest.astype(jnp.bfloat16)
            if piece < 2:
                rest = rest - coarse.astype(jnp.float32)
            term = jnp.dot(coarse, filters[half], preferred_element_type=jnp.float32)
            total = term if total is None else total + term
    texture[...] = total * 255.0

    def looked_up(sample):
        level = jnp.clip(sample, 0.0, 255.0)
        index = jnp.minimum(level.astype(jnp.int32), 254)
        fraction = level - index.astype(jnp.float32)
        place = index & (LANES - 1)
        upper_half = index >= LANES

        def pick(first):
            one = jnp.take_along_axis(words[first], place, axis=1, mode="promise_in_bounds")
            two = jnp.take_along_axis(words[first + 1], place, axis=1, mode="promise_in_bounds")
            return jnp.where(upper_half, two, one)

        def channels(value):
            spread = [value & 255, lax.shift_right_logical(value, 8) & 255, lax.shift_right_logical(value, 16) & 255,
                      lax.shift_right_logical(value, 24)]
            return [channel.astype(jnp.float32) for channel in spread]

        return channels(pick(0)), channels(pick(2)), fraction

    def peer_at(step):
        return lax.rem(my_depth + step, n_depth)

    def part_copy(step):
        peer = peer_at(step)
        return pltpu.make_async_remote_copy(
            src_ref=part.at[peer], dst_ref=mixed.at[my_depth], send_sem=part_send.at[step],
            recv_sem=part_recv.at[my_depth], device_id={"depth": peer}, device_id_type=MESH)

    def part_arrival(step):
        peer = peer_at(step)
        return pltpu.make_async_remote_copy(
            src_ref=part.at[peer], dst_ref=mixed.at[peer], send_sem=part_send.at[step],
            recv_sem=part_recv.at[peer], device_id={"depth": peer}, device_id_type=MESH)

    def final_copy(step):
        peer = peer_at(step)
        return pltpu.make_async_remote_copy(
            src_ref=final.at[my_depth], dst_ref=final.at[my_depth], send_sem=fin_send.at[step],
            recv_sem=fin_recv.at[my_depth], device_id={"depth": peer}, device_id_type=MESH)

    def final_arrival(step):
        peer = peer_at(step)
        return pltpu.make_async_remote_copy(
            src_ref=final.at[peer], dst_ref=final.at[peer], send_sem=fin_send.at[step],
            recv_sem=fin_recv.at[peer], device_id={"depth": peer}, device_id_type=MESH)

    def rendered(block):
        base = row_base(block)
        samples = []
        for pair in range(8):
            sample = None
            for i in range(4):
                term = weights[block, pair, i] * texture[pl.ds(pair * NR + base + i, 1), :]
                sample = term if sample is None else sample + term
            samples.append(sample)
        clear = jnp.ones((8, LANES), jnp.float32)
        sums = [jnp.zeros((8, LANES), jnp.float32) for _ in range(3)]
        for k in range(8):
            below, above, fraction = looked_up(jnp.where(lowest_first, samples[k], samples[7 - k]))
            alpha = (below[3] + (above[3] - below[3]) * fraction) * (6.0 / SLICES / 255.0)
            weight = clear * alpha
            share = weight * fraction
            keep = weight - share
            for c in range(3):
                sums[c] = sums[c] + (keep * below[c] + share * above[c])
            clear = clear - weight
        sums = [value * (1.0 / 255.0) for value in sums] + [1.0 - clear]
        turned = [pltpu.roll(value, PIX, 1) for value in sums]
        front_alpha = jnp.where(first_half_front, sums[3], turned[3])
        pieces = []
        for c in (0, 2):
            near = jnp.where(near_half, sums[c], turned[c + 1])
            far = jnp.where(near_half, turned[c], sums[c + 1])
            front = jnp.where(lowest_first, near, far)
            back = jnp.where(lowest_first, far, near)
            pieces.append(front + (1.0 - front_alpha) * back)
        return pieces

    for steps in ((4,), (3, 5), (2, 6), (1, 7, 0)):
        for step in steps:
            block = peer_at(step)
            pieces = rendered(block)
            for i in range(2):
                if step:
                    part[block, i] = pieces[i]
                else:
                    mixed[my_depth, i] = pieces[i]
        if steps[0] == 4:
            for side in range(2):
                pl.semaphore_wait(token.at[side], 1)
        for step in steps:
            if step:
                part_copy(step).start()

    columns_part(ext1, 2)
    first_stage(2)

    for step in range(1, n_depth):
        part_arrival(step).wait_recv()
    clear = jnp.ones((8, LANES), jnp.float32)
    sums = [jnp.zeros((8, LANES), jnp.float32) for _ in range(2)]
    for k in range(n_depth):
        pair = [jnp.where(lowest_first, mixed[k, i], mixed[n_depth - 1 - k, i]) for i in range(2)]
        alpha = jnp.where(near_half, pltpu.roll(pair[1], PIX, 1), pair[1])
        sums = [total + clear * value for total, value in zip(sums, pair)]
        clear = clear * (1.0 - alpha)
    for i in range(2):
        final[my_depth, i] = sums[i]
    for step in (4, 3, 5, 2, 6, 1, 7):
        final_copy(step).start()
    for f in FIELDS[1:3]:
        columns_part(ext2, f)
        second_stage(f)
    columns_part(ext2, 2)
    second_stage(2)
    for stage in range(2):
        for f in FIELDS:
            for copy in face_copies(stage, f) + column_copies(stage, f):
                copy.wait_send()
    for step in range(1, n_depth):
        part_copy(step).wait_send()
    for step in range(1, n_depth):
        final_arrival(step).wait_recv()
    for step in range(1, n_depth):
        final_copy(step).wait_send()


def finish(out, final, new_state, image, tile, sem, tile_sem):
    copies = [pltpu.make_async_copy(out.at[f], new_state.at[f], sem.at[f]) for f in range(4)]
    for copy in copies:
        copy.start()
    for block in range(8):
        for i in range(2):
            value = final[block, i]
            tile[2 * i, 8 * block : 8 * block + 8, :] = value[:, :PIX]
            tile[2 * i + 1, 8 * block : 8 * block + 8, :] = value[:, PIX:]
    copies.append(pltpu.make_async_copy(tile, image, tile_sem))
    copies[4].start()
    for copy in copies:
        copy.wait()


def solution(mesh):
    sizes = tuple(mesh.shape[axis] for axis in ("depth", "row", "col"))
    f32 = jnp.float32
    any_space = pl.BlockSpec(memory_space=pl.ANY)
    hbm = pl.BlockSpec(memory_space=pltpu.HBM)
    vmem = pl.BlockSpec(memory_space=pltpu.VMEM)
    extended = (4, ND + 8, NR + 16, LANES)

    def local(state, velocity, view_order, tf_table):
        held = pl.pallas_call(
            functools.partial(kernel, sizes),
            out_shape=(pltpu.VMEM((4, ND, NR, LANES), f32), pltpu.VMEM((8, 2, 8, LANES), f32)),
            in_specs=[any_space, any_space, hbm, hbm],
            out_specs=(vmem, vmem),
            scratch_shapes=[
                pltpu.VMEM(extended, f32),
                pltpu.VMEM(extended, f32),
                pltpu.VMEM((3, ND, NR, LANES), f32),
                pltpu.VMEM((2, ND, NR, LANES), f32),
                pltpu.VMEM((4, ND, NR, LANES), f32),
                pltpu.VMEM((2, 4, NR, LANES), f32),
                pltpu.VMEM((2, 2, 4, NR, LANES), f32),
                pltpu.VMEM((NR, LANES), f32),
                pltpu.VMEM((8, 8, 4, 8, LANES), f32),
                pltpu.VMEM((2, LANES, LANES), jnp.bfloat16),
                pltpu.VMEM((4, 8, LANES), jnp.int32),
                pltpu.VMEM((1, 1), jnp.int32),
                pltpu.VMEM((4, 2 * LANES), jnp.int32),
                pltpu.VMEM((LANES, LANES), f32),
                pltpu.VMEM((8, 2, 8, LANES), f32),
                pltpu.VMEM((8, 2, 8, LANES), f32),
                pltpu.SemaphoreType.DMA((4,)),
                pltpu.SemaphoreType.DMA,
                pltpu.SemaphoreType.DMA((2,)),
                pltpu.SemaphoreType.DMA((2, 4, 6)),
                pltpu.SemaphoreType.DMA((2, 4, 6)),
                pltpu.SemaphoreType.DMA((8,)),
                pltpu.SemaphoreType.DMA((8,)),
                pltpu.SemaphoreType.DMA((8,)),
                pltpu.SemaphoreType.DMA((8,)),
                pltpu.SemaphoreType.REGULAR((2,)),
            ],
            compiler_params=pltpu.CompilerParams(collective_id=0, has_side_effects=True),
        )(state, velocity, view_order, tf_table)
        return tuple(pl.pallas_call(
            finish,
            out_shape=(
                jax.ShapeDtypeStruct((4, ND, NR, LANES), f32),
                jax.ShapeDtypeStruct((4, PIX, PIX), f32),
            ),
            in_specs=[vmem, vmem],
            out_specs=(any_space, any_space),
            scratch_shapes=[pltpu.VMEM((4, PIX, PIX), f32), pltpu.SemaphoreType.DMA((4,)), pltpu.SemaphoreType.DMA],
        )(*(pltpu.with_memory_space_constraint(value, pltpu.VMEM) for value in held)))

    return jax.shard_map(
        local,
        mesh=mesh,
        in_specs=(P(None, "depth", "row", "col"), P(None, "depth", "row", "col"), P("row", "col"), P()),
        out_specs=(P(None, "depth", "row", "col"), P(None, "row", "col")),
        check_vma=False,
    )
```
